32 devices in a mesh: stream: 4 (over y, x), replica: 8 (over z, core).
Axes of the slice: x: 2, y: 2, z: 4, core: 2. Of those that a mesh axis runs over, the one named last changes fastest.
Arguments:
- query_embeds: bfloat16 [64, 32, 384], P(('stream', 'replica')), may hold values from -6 to 6
- doc_embeds: bfloat16 [32, 512, 384], P(('stream', 'replica')), may hold values from -6 to 6
- doc_segments: int32 [32, 512], P(('stream', 'replica')), may hold values from 0 to 3, never falling along the last dimension, each value on 1 to 256 neighbouring positions
- candidates: int32 [64, 16], replicated, may hold values from 0 to 127, all different within a row; in each aligned block of 64 rows (0 to 63, 64 to 127, ...) at most 32 rows name the same one
- neg_counts: int32 [64], replicated, may hold values from 1 to 15
- w_qkv: float32 [384, 1152], replicated, may hold values from -0.3125 to 0.3125
- w_out: float32 [384, 384], replicated, may hold values from -1.25 to 1.25
- w_up: float32 [384, 1536], replicated, may hold values from -0.3125 to 0.3125
- w_down: float32 [1536, 384], replicated, may hold values from -0.15625 to 0.15625
- w_head: float32 [384, 96], replicated, may hold values from -0.3125 to 0.3125
- vectors: float32 [5088], replicated, may hold values from -2 to 2, as said below
- mom_qkv: float32 [384, 1152], replicated, may hold values from -6 to 6
- mom_out: float32 [384, 384], replicated, may hold values from -6 to 6
- mom_up: float32 [384, 1536], replicated, may hold values from -6 to 6
- mom_down: float32 [1536, 384], replicated, may hold values from -6 to 6
- mom_head: float32 [384, 96], replicated, may hold values from -6 to 6
- mom_vectors: float32 [5088], replicated, may hold values from -6 to 6
- err_qkv: float32 [8, 384, 1152], P('replica'), may hold values from -3.5 to 3.5
- err_out: float32 [8, 384, 384], P('replica'), may hold values from -3.5 to 3.5
- err_up: float32 [8, 384, 1536], P('replica'), may hold values from -3.5 to 3.5
- err_down: float32 [8, 1536, 384], P('replica'), may hold values from -3.5 to 3.5
- err_head: float32 [8, 384, 96], P('replica'), may hold values from -3.5 to 3.5
- fac_qkv: float32 [1152, 8], replicated, may hold values from -6 to 6
- fac_out: float32 [384, 8], replicated, may hold values from -6 to 6
- fac_up: float32 [1536, 8], replicated, may hold values from -6 to 6
- fac_down: float32 [384, 8], replicated, may hold values from -6 to 6
- fac_head: float32 [96, 8], replicated, may hold values from -6 to 6
Outputs:
- loss: float32 [], replicated
- new_qkv: float32 [384, 1152], replicated
- new_out: float32 [384, 384], replicated
- new_up: float32 [384, 1536], replicated
- new_down: float32 [1536, 384], replicated
- new_head: float32 [384, 96], replicated
- new_vectors: float32 [5088], replicated
- newmom_qkv: float32 [384, 1152], replicated
- newmom_out: float32 [384, 384], replicated
- newmom_up: float32 [384, 1536], replicated
- newmom_down: float32 [1536, 384], replicated
- newmom_head: float32 [384, 96], replicated
- newmom_vectors: float32 [5088], replicated
- newerr_qkv: float32 [8, 384, 1152], P('replica')
- newerr_out: float32 [8, 384, 384], P('replica')
- newerr_up: float32 [8, 384, 1536], P('replica')
- newerr_down: float32 [8, 1536, 384], P('replica')
- newerr_head: float32 [8, 384, 96], P('replica')
- newfac_qkv: float32 [1152, 8], replicated
- newfac_out: float32 [384, 8], replicated
- newfac_up: float32 [1536, 8], replicated
- newfac_down: float32 [384, 8], replicated
- newfac_head: float32 [96, 8], replicated
The draws below stay inside these ranges and needn't reach their ends.
Inputs may be any that keep to these rules, and one draw needn't show every extreme that they name: `doc_segments`: each row holds all 4 documents in order, each 1 to 256 tokens, one of exactly 256. `candidates`: A query's 16 ids are distinct; no document is named by more than 32 queries, a bound that some block reaches. `vectors`: gains lie near one, biases near zero.
All inputs are finite; a program needn't handle non-finite values.
Results may differ from the reference program's by a relative error of at most 0.0004.
Values may be sent and summed in bfloat16 or wider, within the bound.
No kernel may reach another device: no remote copies, remote signals or barrier semaphores. Data moves between devices by JAX's collectives and lax.ppermute only.
A program may use at most 192 MiB of HBM per device.

```python
import math
import jax
import jax.numpy as jnp
import numpy as np
from jax import lax

D = 384
HEADS = 12
HDIM = 32
FF = 1536
PDIM = 96
RANK = 8
QLEN = 32
NCAND = 16
NSEG = 4
QDEV = 2
ROW = 512
SEGMOST = 256
MOSTQ = 32
ROWS = 32
QUERIES = 64
NDOCS = 128
VEC = 5088
N_STREAM = 4
N_REPLICA = 8


def draw_vectors(key, part):
    keys = jax.random.split(key, 2)
    biases = 0.3 * jax.random.normal(keys[0], (VEC,), jnp.float32)
    gains = jax.random.uniform(keys[1], (VEC,), jnp.float32, 0.6, 1.4)
    places = jnp.arange(VEC)
    start = 5 * D + FF
    is_gain = (places >= start) & (places < start + D) | (places >= start + 2 * D) & (places < start + 3 * D)
    return jnp.clip(jnp.where(is_gain, gains, biases), -2.0, 2.0)


def place_ends(entries, rng, smallest, high):
    longest = entries.shape.index(max(entries.shape))
    spots = []
    for shift in (0, 1):
        where = [jax.random.randint(jax.random.fold_in(rng, axis), (), 0, length) for axis, length in enumerate(entries.shape)]
        where[longest] = (where[longest] + shift) % entries.shape[longest]
        spots.append(tuple(where))
    return entries.at[spots[0]].set(smallest).at[spots[1]].set(high)


def level_of(key, extent, cuts, smallest, largest):
    level = 1.0
    for dim, shards_of in cuts:
        draws = jax.random.uniform(jax.random.fold_in(jax.random.fold_in(key, 6), dim), (shards_of,), jnp.float32, smallest / len(cuts), largest / len(cuts))
        level = level * jnp.repeat(jnp.exp(draws), extent[dim] // shards_of).reshape((-1,) + (1,) * (len(extent) - 1 - dim))
    return level


def profile(amount, total, reach, skew):
    loads = [(1 << 20) // math.isqrt(rank ** skew) + 1 for rank in range(2, amount + 1)]
    spare, given = total - reach - (amount - 1), [1] * (amount - 1)
    while spare > 0:
        free = [i for i in range(amount - 1) if given[i] < reach]
        pool, left = sum([loads[i] for i in free]), spare
        for i in free:
            more = min(reach - given[i], max(1, left * loads[i] // pool), spare)
            given[i] = given[i] + more
            spare = spare - more
    return np.array([reach] + given)


def uneven(key, amount, total, limit, skew):
    if amount == 2:
        one = jax.random.randint(key, (), max(1, total - limit), min(limit, total - 1) + 1)
        return jnp.stack([one, total - one])
    sizes = jnp.asarray(profile(amount, total, limit, skew), jnp.int32)
    twos = (amount - 1) // 2
    donor, sink = sizes[1:1 + 2 * twos:2], sizes[2:2 + 2 * twos:2]
    room = jnp.minimum(donor - 1, limit - sink)
    moved = jax.random.randint(jax.random.fold_in(key, 1), (twos,), 0, 1 << 20) % (room + 1)
    sizes = sizes.at[1:1 + 2 * twos:2].set(donor - moved).at[2:2 + 2 * twos:2].set(sink + moved)
    return sizes[jax.random.permutation(jax.random.fold_in(key, 2), amount)]


def deal_out(key, own, number, rows, count, top, most, lean):
    order = jax.random.permutation(key, count)
    heavy_load, usual = shares(count, rows * top, most, lean, True), shares(count, rows * top, most, lean, False)
    places = jnp.arange(count)

    def named(sizes, turn):
        used = int((sizes > 0).sum())
        fixed = max(1, used // 4)
        passed = fixed + (places - fixed + turn * (used - fixed)) % max(1, count - fixed)
        return jnp.zeros((count,), jnp.int32).at[order[jnp.where(places < fixed, places, passed)]].set(jnp.asarray(sizes, jnp.int32))

    sizes = jnp.where(number % 4 == 0, named(heavy_load, number // 4), named(usual, number - number // 4 - 1))
    mixed = jax.random.permutation(jax.random.fold_in(own, 3), count)
    source_of, taker = mixed[0:count // 2 * 2:2], mixed[1:count // 2 * 2:2]
    slack = jnp.minimum(sizes[source_of] - 1, most - sizes[taker]) // 2
    slack = jnp.where((source_of == order[0]) | (taker == order[0]) | (sizes[taker] == 0), 0, jnp.maximum(slack, 0))
    passed = jax.random.randint(jax.random.fold_in(own, 4), (count // 2,), 0, 1 << 20) % (slack + 1)
    sizes = sizes.at[source_of].add(-passed).at[taker].add(passed)
    members = jnp.searchsorted(jnp.cumsum(sizes), jnp.arange(rows * top), side="right").astype(jnp.int32)
    listing = members.reshape(top, rows).T
    listing = listing[jax.random.permutation(jax.random.fold_in(own, 1), rows)]
    turn = jax.random.randint(jax.random.fold_in(own, 2), (rows, 1), 0, top)
    return jnp.take_along_axis(listing, (jnp.arange(top)[None, :] + turn) % top, axis=1)


def shares(count, total, reach, slope, full):
    loads = [(1 << 20) // math.isqrt(grade ** slope) + 1 for grade in range(1, count + 1)]
    largest = reach if full else min(reach, max(-(-total // count), total * loads[0] // sum(loads)))
    least = 1 if total - largest >= count - 1 else 0
    counts, rest = [largest] + [least] * (count - 1), total - largest - least * (count - 1)
    while rest > 0:
        free = [i for i in range(1, count) if counts[i] < largest] or [i for i in range(1, count) if counts[i] < reach]
        mass, budget = sum([loads[i] for i in free]), rest
        for i in free:
            extra = min(reach - counts[i], max(1, budget * loads[i] // mass), rest)
            counts[i] = counts[i] + extra
            rest = rest - extra
    return np.array(counts)


def normal_values(own_key, extent, spread, limit, shards=(), kind=jnp.bfloat16):
    result = spread * jax.random.normal(own_key, extent, jnp.float32)
    if shards:
        result = result * level_of(own_key, extent, shards, -0.22, 0.18)
    return jnp.clip(result, -limit, limit).astype(kind)


def setup_inputs(seed: int = 0) -> dict:
    streams_of = jax.random.split(jax.random.key(seed), 28)
    query_embeds = normal_values(streams_of[0], (QUERIES, QLEN, D), 1.0, 6.0, ((0, 32),))
    doc_embeds = normal_values(streams_of[1], (ROWS, ROW, D), 1.0, 6.0, ((0, 32),))
    doc_segments = jax.vmap(lambda own: jnp.searchsorted(jnp.cumsum(uneven(own, NSEG, ROW, SEGMOST, 2)), jnp.arange(ROW), side="right"))(jax.random.split(streams_of[2], ROWS)).reshape((ROWS, ROW)).astype(jnp.int32)
    candidates_keys = jax.random.split(jax.random.fold_in(streams_of[3], 1), QUERIES // QUERIES)
    candidates_turns = jax.random.permutation(jax.random.fold_in(streams_of[3], 3), QUERIES // QUERIES)
    candidates = jax.vmap(lambda own, number: deal_out(jax.random.fold_in(streams_of[3], 2), own, number, QUERIES, NDOCS, NCAND, MOSTQ, 2))(candidates_keys, candidates_turns).reshape((QUERIES, NCAND))
    neg_counts = place_ends(jax.random.randint(streams_of[4], (QUERIES,), 1, NCAND), jax.random.fold_in(streams_of[4], 1), 1, NCAND - 1).astype(jnp.int32)
    w_qkv = normal_values(streams_of[5], (D, 3 * D), D ** -0.5, 0.3125, (), jnp.float32)
    w_out = normal_values(streams_of[6], (D, D), (D // 16) ** -0.5, 1.25, (), jnp.float32)
    w_up = normal_values(streams_of[7], (D, FF), D ** -0.5, 0.3125, (), jnp.float32)
    w_down = normal_values(streams_of[8], (FF, D), FF ** -0.5, 0.15625, (), jnp.float32)
    w_head = normal_values(streams_of[9], (D, PDIM), D ** -0.5, 0.3125, (), jnp.float32)
    vectors = draw_vectors(jax.random.fold_in(streams_of[27], 71), 0)
    mom_qkv = normal_values(streams_of[11], (D, 3 * D), (0.3 * (ROW + QLEN * QDEV) ** 0.5 / (QDEV * (N_STREAM * N_REPLICA) ** 0.5)), 6.0, (), jnp.float32)
    mom_out = normal_values(streams_of[12], (D, D), (0.3 * (ROW + QLEN * QDEV) ** 0.5 / (QDEV * (N_STREAM * N_REPLICA) ** 0.5)), 6.0, (), jnp.float32)
    mom_up = normal_values(streams_of[13], (D, FF), (0.3 * (ROW + QLEN * QDEV) ** 0.5 / (QDEV * (N_STREAM * N_REPLICA) ** 0.5)), 6.0, (), jnp.float32)
    mom_down = normal_values(streams_of[14], (FF, D), (0.3 * (ROW + QLEN * QDEV) ** 0.5 / (QDEV * (N_STREAM * N_REPLICA) ** 0.5)), 6.0, (), jnp.float32)
    mom_head = normal_values(streams_of[15], (D, PDIM), (0.3 * (ROW + QLEN * QDEV) ** 0.5 / (QDEV * (N_STREAM * N_REPLICA) ** 0.5)), 6.0, (), jnp.float32)
    mom_vectors = normal_values(streams_of[16], (VEC,), (0.9 * (ROW + QLEN * QDEV) ** 0.5 / (QDEV * (N_STREAM * N_REPLICA) ** 0.5)), 6.0, (), jnp.float32)
    err_qkv = normal_values(streams_of[17], (N_REPLICA, D, 3 * D), (0.3 * (ROW + QLEN * QDEV) ** 0.5 / (QDEV * (N_STREAM * N_REPLICA) ** 0.5 * N_REPLICA ** 0.5)), 3.5, ((0, 8),), jnp.float32)
    err_out = normal_values(streams_of[18], (N_REPLICA, D, D), (0.3 * (ROW + QLEN * QDEV) ** 0.5 / (QDEV * (N_STREAM * N_REPLICA) ** 0.5 * N_REPLICA ** 0.5)), 3.5, ((0, 8),), jnp.float32)
    err_up = normal_values(streams_of[19], (N_REPLICA, D, FF), (0.3 * (ROW + QLEN * QDEV) ** 0.5 / (QDEV * (N_STREAM * N_REPLICA) ** 0.5 * N_REPLICA ** 0.5)), 3.5, ((0, 8),), jnp.float32)
    err_down = normal_values(streams_of[20], (N_REPLICA, FF, D), (0.3 * (ROW + QLEN * QDEV) ** 0.5 / (QDEV * (N_STREAM * N_REPLICA) ** 0.5 * N_REPLICA ** 0.5)), 3.5, ((0, 8),), jnp.float32)
    err_head = normal_values(streams_of[21], (N_REPLICA, D, PDIM), (0.3 * (ROW + QLEN * QDEV) ** 0.5 / (QDEV * (N_STREAM * N_REPLICA) ** 0.5 * N_REPLICA ** 0.5)), 3.5, ((0, 8),), jnp.float32)
    fac_qkv = normal_values(streams_of[22], (3 * D, RANK), 1.0, 6.0, (), jnp.float32)
    fac_out = normal_values(streams_of[23], (D, RANK), 1.0, 6.0, (), jnp.float32)
    fac_up = normal_values(streams_of[24], (FF, RANK), 1.0, 6.0, (), jnp.float32)
    fac_down = normal_values(streams_of[25], (D, RANK), 1.0, 6.0, (), jnp.float32)
    fac_head = normal_values(streams_of[26], (PDIM, RANK), 1.0, 6.0, (), jnp.float32)
    return dict(query_embeds=query_embeds, doc_embeds=doc_embeds, doc_segments=doc_segments, candidates=candidates, neg_counts=neg_counts, w_qkv=w_qkv, w_out=w_out, w_up=w_up, w_down=w_down, w_head=w_head, vectors=vectors, mom_qkv=mom_qkv, mom_out=mom_out, mom_up=mom_up, mom_down=mom_down, mom_head=mom_head, mom_vectors=mom_vectors, err_qkv=err_qkv, err_out=err_out, err_up=err_up, err_down=err_down, err_head=err_head, fac_qkv=fac_qkv, fac_out=fac_out, fac_up=fac_up, fac_down=fac_down, fac_head=fac_head)


HIGH = lax.Precision.HIGHEST
SOFT = 0.03
MOMENTUM = 0.9
RATE = 0.1

@jax.custom_vjp
def low(v):
    return lax.optimization_barrier(v.astype(jnp.bfloat16)).astype(jnp.float32)

@jax.custom_vjp
def low_back(v):
    return v

def low_keep(v):
    return (low(v), None)

def low_pass(kept, grad):
    return (grad,)

def back_keep(v):
    return (v, None)

def back_low(kept, grad):
    return (low(grad),)
low.defvjp(low_keep, low_pass)
low_back.defvjp(back_keep, back_low)

def split_vec(packed):
    return jnp.split(packed, [3 * D, 4 * D, 4 * D + FF, 5 * D + FF, 6 * D + FF, 7 * D + FF, 8 * D + FF, 9 * D + FF])

def layer_norm(resid, gain, shift):
    center = resid - lax.optimization_barrier(jnp.mean(resid, -1, keepdims=True))
    return center * lax.rsqrt(lax.optimization_barrier(jnp.mean(center * center, -1, keepdims=True)) + 1e-05) * gain + shift

def gelu(value):
    return 0.5 * value * (1.0 + jax.scipy.special.erf(value * 0.7071067811865476))

def rotary(value, cosine, sine):
    half = value.shape[-1] // 2
    return value * cosine + jnp.concatenate([-value[..., half:], value[..., :half]], -1) * sine

def tables(segment):
    count = segment.shape[0]
    places = jnp.arange(count)
    same = segment[:, None] == segment[None, :]
    position = lax.optimization_barrier(jnp.sum(same & (places[None, :] < places[:, None]), 1)).astype(jnp.float32)
    freqs = 10000.0 ** (-(jnp.arange(HDIM // 2).astype(jnp.float32) * 2.0) / HDIM)
    angle = position[:, None] * freqs[None, :]
    cosine = jnp.concatenate([jnp.cos(angle), jnp.cos(angle)], -1)[:, None, :]
    sine = jnp.concatenate([jnp.sin(angle), jnp.sin(angle)], -1)[:, None, :]
    return (same, cosine, sine)

def encode(params, tokens_in, same, cosine, sine):
    w_qkv, w_out, w_up, w_down, w_head, packed = params
    b_qkv, b_out, b_up, b_down, gain_one, shift_one, gain_two, shift_two, b_head = split_vec(packed)
    count = tokens_in.shape[0]
    qkv = low_back(jnp.dot(tokens_in, low(w_qkv), precision=HIGH)) + b_qkv
    qkv = qkv.reshape(count, 3, HEADS, HDIM)
    queries = rotary(qkv[:, 0], cosine, sine)
    keys_rot = rotary(qkv[:, 1], cosine, sine)
    values = qkv[:, 2]
    scores = low_back(jnp.einsum('ihd,jhd->hij', low(queries), low(keys_rot), precision=HIGH) * HDIM ** (-0.5))
    scores = jnp.where(same[None], scores, -1e+30)
    probs = jax.nn.softmax(scores, axis=-1)
    context = jnp.einsum('hij,jhd->ihd', low(probs), low(values), precision=HIGH).reshape(count, D)
    context = low(low_back(context))
    attended = low_back(jnp.dot(context, low(w_out), precision=HIGH)) + b_out
    hidden_one = layer_norm(tokens_in + attended, gain_one, shift_one)
    inner = low_back(jnp.dot(low(hidden_one), low(w_up), precision=HIGH)) + b_up
    mixed = low_back(jnp.dot(low(gelu(inner)), low(w_down), precision=HIGH)) + b_down
    hidden_two = layer_norm(hidden_one + mixed, gain_two, shift_two)
    emitted = low_back(jnp.dot(low(hidden_two), low(w_head), precision=HIGH)) + b_head
    return emitted * lax.rsqrt(lax.optimization_barrier(jnp.sum(emitted * emitted, -1, keepdims=True)) + 1e-06)

def maxsim_row(query_vecs, doc_vecs, segment):
    segmask = segment[None, :] == jnp.arange(NSEG)[:, None]
    block_rows = math.gcd(QUERIES * QLEN, 512)

    def block(rows):
        sim = low_back(jnp.dot(rows, doc_vecs.T, precision=HIGH)) / SOFT
        masked = jnp.where(segmask[None], sim[:, None, :], -1e+30)
        return SOFT * jax.nn.logsumexp(masked, -1)
    parts = lax.map(jax.checkpoint(block), query_vecs.reshape(-1, block_rows, PDIM))
    return parts.reshape(QUERIES, QLEN, NSEG).sum(1)

def orthogonal(left):
    columns = []
    for number in range(left.shape[1]):
        column = left[:, number]
        for before in columns:
            column = column - jnp.sum(before * column) * before
        column = column * lax.rsqrt(jnp.sum(column * column) + 1e-12)
        columns.append(column)
    return jnp.stack(columns, 1)

def reference(query_embeds, doc_embeds, doc_segments, candidates, neg_counts, w_qkv, w_out, w_up, w_down, w_head, vectors, mom_qkv, mom_out, mom_up, mom_down, mom_head, mom_vectors, err_qkv, err_out, err_up, err_down, err_head, fac_qkv, fac_out, fac_up, fac_down, fac_head):
    qtok = QDEV * QLEN
    tokens_in = jnp.concatenate([doc_embeds, query_embeds.reshape(ROWS, qtok, D)], 1).astype(jnp.float32)
    query_seg = jnp.broadcast_to(NSEG + jnp.arange(qtok) // QLEN, (ROWS, qtok)).astype(jnp.int32)
    segs = jnp.concatenate([doc_segments.astype(jnp.int32), query_seg], 1)
    same, cosine, sine = jax.vmap(tables)(segs)
    params = (w_qkv, w_out, w_up, w_down, w_head, vectors)
    stacked = tuple((jnp.broadcast_to(p, (ROWS,) + p.shape) for p in params))

    def loss_fn(stacked_params):
        vecs = lax.map(lambda a: jax.checkpoint(encode)(a[0], a[1], a[2], a[3], a[4]), (stacked_params, tokens_in, same, cosine, sine))
        vecs = low(vecs)
        doc_vecs = vecs[:, :ROW]
        query_vecs = vecs[:, ROW:].reshape(QUERIES * QLEN, PDIM)
        scores = lax.map(lambda a: maxsim_row(query_vecs, a[0], a[1]), (doc_vecs, doc_segments))
        table = jnp.transpose(scores, (1, 0, 2)).reshape(QUERIES, NDOCS)
        picked = jnp.take_along_axis(table, candidates, 1)
        valid = jnp.arange(NCAND)[None, :] <= neg_counts[:, None]
        logits = jnp.where(valid, picked, -1e+30)
        return jnp.mean(jax.nn.logsumexp(logits, -1) - logits[:, 0])
    loss, pull = jax.vjp(loss_fn, stacked)
    grads = pull(jnp.ones((), loss.dtype))[0]
    summed = tuple((g.reshape((N_STREAM, N_REPLICA) + g.shape[1:]).sum(0) for g in grads))
    rate = RATE * QDEV * math.sqrt(ROWS / (ROW + QLEN * QDEV))
    moms = (mom_qkv, mom_out, mom_up, mom_down, mom_head)
    errs = (err_qkv, err_out, err_up, err_down, err_head)
    facs = (fac_qkv, fac_out, fac_up, fac_down, fac_head)
    new_w, new_m, new_e, new_f = ([], [], [], [])
    for number in range(5):
        merged = summed[number] + errs[number]
        left = jnp.einsum('rmn,nk->mk', merged, facs[number], precision=HIGH)
        basis = orthogonal(left)
        right = jnp.einsum('rmn,mk->nk', merged, basis, precision=HIGH)
        approx = jnp.dot(basis, right.T, precision=HIGH)
        new_e.append(merged - approx[None] / N_REPLICA)
        momentum = MOMENTUM * moms[number] + approx
        new_m.append(momentum)
        new_w.append(params[number] - rate * momentum)
        new_f.append(right)
    vec_mom = MOMENTUM * mom_vectors + summed[5].sum(0)
    new_vec = vectors - rate * vec_mom
    return (loss, new_w[0], new_w[1], new_w[2], new_w[3], new_w[4], new_vec, new_m[0], new_m[1], new_m[2], new_m[3], new_m[4], vec_mom, new_e[0], new_e[1], new_e[2], new_e[3], new_e[4], new_f[0], new_f[1], new_f[2], new_f[3], new_f[4])
```

```python
import math

import jax
import jax.numpy as jnp
from jax import lax
from jax.experimental import pallas as pl
from jax.sharding import PartitionSpec as P

D = 384
HEADS = 12
HDIM = 32
FF = 1536
NSEG = 4


HIGH = lax.Precision.HIGHEST
SOFT = 0.03
MOMENTUM = 0.9
RATE = 0.1


def split_vec(packed):
    return jnp.split(
        packed,
        [3 * D, 4 * D, 4 * D + FF, 5 * D + FF, 6 * D + FF, 7 * D + FF, 8 * D + FF, 9 * D + FF],
    )


def inner(first, second):
    return lax.dot_general(
        first, second, (((0,), (0,)), ((), ())), preferred_element_type=jnp.float32
    )


def layer_norm(resid, gain, shift):
    center = resid - jnp.mean(resid, -1, keepdims=True)
    inv_std = lax.rsqrt(jnp.mean(center * center, -1, keepdims=True) + 1e-05)
    normed = center * inv_std
    return (normed * gain + shift, normed, inv_std)


def norm_back(grad_out, gain, normed, inv_std):
    scaled = grad_out * gain
    grad_in = inv_std * (
        scaled
        - jnp.mean(scaled, -1, keepdims=True)
        - normed * jnp.mean(scaled * normed, -1, keepdims=True)
    )
    return (grad_in, jnp.sum(grad_out * normed, 0), jnp.sum(grad_out, 0))


def gelu(value):
    return 0.5 * value * (1.0 + jax.scipy.special.erf(value * 0.7071067811865476))


def gelu_slope(value):
    return (
        0.5 * (1.0 + jax.scipy.special.erf(value * 0.7071067811865476))
        + value * jnp.exp(-0.5 * value * value) * 0.3989422804014327
    )


def rotary(value, cosine, sine):
    half = value.shape[-1] // 2
    return value * cosine + jnp.concatenate([-value[..., half:], value[..., :half]], -1) * sine


def rotary_back(grad, cosine, sine):
    half = grad.shape[-1] // 2
    turned = grad * sine
    return grad * cosine + jnp.concatenate([turned[..., half:], -turned[..., :half]], -1)


def tables(segment):
    count = segment.shape[0]
    places = jnp.arange(count)
    same = segment[:, None] == segment[None, :]
    position = jnp.sum(same & (places[None, :] < places[:, None]), 1).astype(jnp.float32)
    freqs = 10000.0 ** (-(jnp.arange(HDIM // 2).astype(jnp.float32) * 2.0) / HDIM)
    angle = position[:, None] * freqs[None, :]
    cosine = jnp.concatenate([jnp.cos(angle), jnp.cos(angle)], -1)[:, None, :]
    sine = jnp.concatenate([jnp.sin(angle), jnp.sin(angle)], -1)[:, None, :]
    return (same, cosine, sine)


def encode(tokens_in, same, cosine, sine, mats, packed):
    w_qkv, w_out, w_up, w_down, w_head = mats
    b_qkv, b_out, b_up, b_down, gain_one, shift_one, gain_two, shift_two, b_head = split_vec(packed)
    count = tokens_in.shape[0]
    scale = HDIM ** (-0.5)
    qkv = (jnp.dot(tokens_in, w_qkv, preferred_element_type=jnp.float32) + b_qkv).reshape(
        count, 3, HEADS, HDIM
    )
    queries = rotary(qkv[:, 0], cosine, sine).astype(jnp.bfloat16)
    keys_rot = rotary(qkv[:, 1], cosine, sine).astype(jnp.bfloat16)
    values = qkv[:, 2].astype(jnp.bfloat16)
    scores = (
        jnp.einsum("ihd,jhd->hij", queries, keys_rot, preferred_element_type=jnp.float32) * scale
    )
    scores = jnp.where(same[None], scores, -1e30)
    expo = jnp.exp(scores - jnp.max(scores, -1, keepdims=True))
    probs = expo / jnp.sum(expo, -1, keepdims=True)
    probs_low = probs.astype(jnp.bfloat16)
    context = (
        jnp.einsum("hij,jhd->ihd", probs_low, values, preferred_element_type=jnp.float32)
        .reshape(count, D)
        .astype(jnp.bfloat16)
    )
    attended = jnp.dot(context, w_out, preferred_element_type=jnp.float32) + b_out
    hidden_one, normed_one, inv_one = layer_norm(
        tokens_in.astype(jnp.float32) + attended, gain_one, shift_one
    )
    hidden_low = hidden_one.astype(jnp.bfloat16)
    pre_act = jnp.dot(hidden_low, w_up, preferred_element_type=jnp.float32) + b_up
    act_low = gelu(pre_act).astype(jnp.bfloat16)
    mixed = jnp.dot(act_low, w_down, preferred_element_type=jnp.float32) + b_down
    hidden_two, normed_two, inv_two = layer_norm(hidden_one + mixed, gain_two, shift_two)
    second_low = hidden_two.astype(jnp.bfloat16)
    emitted = jnp.dot(second_low, w_head, preferred_element_type=jnp.float32) + b_head
    inv_len = lax.rsqrt(jnp.sum(emitted * emitted, -1, keepdims=True) + 1e-06)
    output = emitted * inv_len
    kept = (
        queries,
        keys_rot,
        values,
        probs,
        probs_low,
        context,
        normed_one,
        inv_one,
        hidden_low,
        pre_act,
        act_low,
        normed_two,
        inv_two,
        second_low,
        inv_len,
        output,
    )
    return (output, kept)


def backward(grad_vec, tokens_in, cosine, sine, kept, mats, packed):
    w_qkv, w_out, w_up, w_down, w_head = mats
    b_qkv, b_out, b_up, b_down, gain_one, shift_one, gain_two, shift_two, b_head = split_vec(packed)
    (
        queries,
        keys_rot,
        values,
        probs,
        probs_low,
        context,
        normed_one,
        inv_one,
        hidden_low,
        pre_act,
        act_low,
        normed_two,
        inv_two,
        second_low,
        inv_len,
        output,
    ) = kept
    count = tokens_in.shape[0]
    scale = HDIM ** (-0.5)
    grad_emit = inv_len * (grad_vec - output * jnp.sum(grad_vec * output, -1, keepdims=True))
    emit_low = grad_emit.astype(jnp.bfloat16)
    grad_hidden_two = jnp.dot(emit_low, w_head.T, preferred_element_type=jnp.float32)
    grad_resid_two, grad_gain_two, grad_shift_two = norm_back(
        grad_hidden_two, gain_two, normed_two, inv_two
    )
    mixed_low = grad_resid_two.astype(jnp.bfloat16)
    grad_act = jnp.dot(mixed_low, w_down.T, preferred_element_type=jnp.float32)
    grad_pre = grad_act * gelu_slope(pre_act)
    pre_low = grad_pre.astype(jnp.bfloat16)
    grad_hidden_one = grad_resid_two + jnp.dot(pre_low, w_up.T, preferred_element_type=jnp.float32)
    grad_resid_one, grad_gain_one, grad_shift_one = norm_back(
        grad_hidden_one, gain_one, normed_one, inv_one
    )
    attn_low = grad_resid_one.astype(jnp.bfloat16)
    grad_context = (
        jnp.dot(attn_low, w_out.T, preferred_element_type=jnp.float32)
        .reshape(count, HEADS, HDIM)
        .astype(jnp.bfloat16)
    )
    grad_probs = jnp.einsum(
        "ihd,jhd->hij", grad_context, values, preferred_element_type=jnp.float32
    )
    grad_values = jnp.einsum(
        "hij,ihd->jhd", probs_low, grad_context, preferred_element_type=jnp.float32
    )
    grad_scores = probs * (grad_probs - jnp.sum(grad_probs * probs, -1, keepdims=True))
    scores_low = grad_scores.astype(jnp.bfloat16)
    grad_queries = (
        jnp.einsum("hij,jhd->ihd", scores_low, keys_rot, preferred_element_type=jnp.float32) * scale
    )
    grad_keys = (
        jnp.einsum("hij,ihd->jhd", scores_low, queries, preferred_element_type=jnp.float32) * scale
    )
    grad_queries = rotary_back(grad_queries, cosine, sine)
    grad_keys = rotary_back(grad_keys, cosine, sine)
    grad_qkv_act = jnp.stack([grad_queries, grad_keys, grad_values], 1).reshape(count, 3 * D)
    grad_packed = jnp.concatenate(
        [
            jnp.sum(grad_qkv_act, 0),
            jnp.sum(grad_resid_one, 0),
            jnp.sum(grad_pre, 0),
            jnp.sum(grad_resid_two, 0),
            grad_gain_one,
            grad_shift_one,
            grad_gain_two,
            grad_shift_two,
            jnp.sum(grad_emit, 0),
        ]
    )
    pairs = (
        (tokens_in, grad_qkv_act.astype(jnp.bfloat16)),
        (context, attn_low),
        (hidden_low, pre_low),
        (act_low, mixed_low),
        (second_low, emit_low),
    )
    return (pairs, grad_packed)


def peers(number):
    return [[(i, i ^ k) for i in range(number)] for k in range(number)]


def spread(value, axis):
    turns = peers(lax.axis_size(axis))
    return jnp.stack([value] + [lax.ppermute(value, axis, turn) for turn in turns[1:]], 0)


def fold(value, axis):
    turns = peers(lax.axis_size(axis))
    total = value[0]
    for k, turn in enumerate(turns):
        if k:
            total = total + lax.ppermute(value[k], axis, turn)
    return total


def all_sum(value):
    axes = ("stream", "replica")
    count = lax.axis_size("stream") * lax.axis_size("replica")
    rows, cols = value.shape
    pieces = value.reshape(rows, count, cols // count).transpose(1, 0, 2)
    got = lax.all_to_all(pieces, axes, 0, 0, tiled=True)
    mine = jnp.sum(got, 0)
    back = lax.all_to_all(
        jnp.broadcast_to(mine[None], pieces.shape), axes, 0, 0, tiled=True
    )
    return back.transpose(1, 0, 2).reshape(rows, cols)


def thirds(value):
    high = lax.reduce_precision(value, 8, 7)
    rest = value - high
    mid = lax.reduce_precision(rest, 8, 7)
    low = rest - mid
    return [part.astype(jnp.bfloat16) for part in (high, mid, low)]


def exact(left, right, contract):
    out = lax.dot_general(
        jnp.concatenate(thirds(left), 0), right, (contract, ((), ())),
        preferred_element_type=jnp.float32,
    )
    return out[:8] + out[8:16] + out[16:]


def basis_kernel(bounds, left_ref, out_ref):
    blocks = [left_ref[:, lo:hi] for lo, hi in bounds]
    places = lax.broadcasted_iota(jnp.int32, (8, 1), 0)
    for turn in range(8):
        for n, block in enumerate(blocks):
            row = block[turn : turn + 1]
            row = row * lax.rsqrt(jnp.sum(row * row, -1, keepdims=True) + 1e-12)
            shares = jnp.sum(block * row, -1, keepdims=True)
            shares = jnp.where(places > turn, shares, 0.0)
            block = block - shares * row
            blocks[n] = jnp.where(places == turn, row, block)
    for (lo, hi), block in zip(bounds, blocks):
        out_ref[:, lo:hi] = block


def shards(
    query_embeds,
    doc_embeds,
    doc_segments,
    candidates,
    neg_counts,
    w_qkv,
    w_out,
    w_up,
    w_down,
    w_head,
    vectors,
    mom_qkv,
    mom_out,
    mom_up,
    mom_down,
    mom_head,
    mom_vectors,
    err_qkv,
    err_out,
    err_up,
    err_down,
    err_head,
    fac_qkv,
    fac_out,
    fac_up,
    fac_down,
    fac_head,
):
    streams, replicas = lax.axis_size("stream"), lax.axis_size("replica")
    devices = streams * replicas
    my_stream, my_replica = lax.axis_index("stream"), lax.axis_index("replica")
    qdev, qlen, width = query_embeds.shape
    row = doc_embeds.shape[1]
    qtok = qdev * qlen
    weights = (w_qkv, w_out, w_up, w_down, w_head)
    moms = (mom_qkv, mom_out, mom_up, mom_down, mom_head)
    errs = (err_qkv[0], err_out[0], err_up[0], err_down[0], err_head[0])
    facs = (fac_qkv, fac_out, fac_up, fac_down, fac_head)
    mats = tuple((w.astype(jnp.bfloat16) for w in weights))
    slot_stream = my_stream ^ jnp.arange(streams)
    slot_replica = my_replica ^ jnp.arange(replicas)
    slot_device = (slot_stream[:, None] * replicas + slot_replica[None, :]).reshape(devices)

    query_in = query_embeds.reshape(qtok, width)
    query_tables = tables(jnp.arange(qtok, dtype=jnp.int32) // qlen)
    query_vecs, query_kept = encode(query_in, *query_tables, mats, vectors)
    query_low = query_vecs.astype(jnp.bfloat16)
    all_query = spread(spread(query_low, "replica"), "stream")

    doc_in = doc_embeds[0]
    doc_tables = tables(doc_segments[0])
    doc_vecs, doc_kept = encode(doc_in, *doc_tables, mats, vectors)
    doc_low = doc_vecs.astype(jnp.bfloat16)
    pdim = doc_low.shape[1]

    tokens = devices * qtok
    rows_all = all_query.reshape(tokens, pdim)
    segment = doc_segments[0]
    sims = (
        lax.dot_general(
            doc_low, rows_all, (((1,), (1,)), ((), ())), preferred_element_type=jnp.float32
        )
        / SOFT
    )
    weight = jnp.exp(sims)
    segmask = (segment[None, :] == jnp.arange(NSEG)[:, None]).astype(jnp.float32)
    totals = jnp.stack(
        [jnp.sum(jnp.where((segment == d)[:, None], weight, 0.0), 0) for d in range(NSEG)], 0
    )
    scores = (SOFT * jnp.log(totals)).reshape(NSEG, devices, qdev, qlen).sum(-1)
    scores = jnp.take(scores, slot_device, axis=1).reshape(NSEG, devices * qdev)
    table = spread(spread(scores, "replica"), "stream").reshape(devices * NSEG, devices * qdev)
    docs = (slot_device[:, None] * NSEG + jnp.arange(NSEG)[None, :]).reshape(-1)
    slots = jnp.arange(candidates.shape[1])
    named = (candidates[None] == docs[:, None, None]) & (slots <= neg_counts[:, None])[None]
    first = (candidates[:, 0][None] == docs[:, None]).astype(jnp.float32)
    listed = jnp.any(named, -1)
    logits = jnp.where(listed, table, -1e30)
    peak = jnp.max(logits, 0, keepdims=True)
    expo = jnp.exp(logits - peak)
    total = jnp.sum(expo, 0, keepdims=True)
    total_queries = candidates.shape[0]
    losses = peak[0] + jnp.log(total[0]) - jnp.sum(table * first, 0)
    loss = jnp.mean(losses)
    grad_table = (expo / total - first) / total_queries
    own = jnp.take(
        grad_table[:NSEG].reshape(NSEG, devices, qdev), slot_device, axis=1
    )
    per_token = jnp.repeat(own.reshape(NSEG, devices * qdev), qlen, axis=1) / totals
    spots = jnp.sum(segmask[:, :, None] * per_token[:, None, :], 0)
    sim_low = (weight * spots).astype(jnp.bfloat16)
    query_grad = lax.dot_general(
        sim_low, doc_low, (((0,), (0,)), ((), ())), preferred_element_type=jnp.float32
    ).reshape(streams, replicas, qtok, pdim)
    query_local = fold(fold(query_grad, "stream"), "replica")
    doc_grad = jnp.dot(sim_low, rows_all, preferred_element_type=jnp.float32)

    doc_pairs, doc_packed = backward(doc_grad, doc_in, *doc_tables[1:], doc_kept, mats, vectors)
    query_pairs, query_packed = backward(
        query_local, query_in, *query_tables[1:], query_kept, mats, vectors
    )
    pairs = [
        (jnp.concatenate([dx, qx], 0), jnp.concatenate([dy, qy], 0))
        for (dx, dy), (qx, qy) in zip(doc_pairs, query_pairs)
    ]
    packed = doc_packed + query_packed
    grads = [lax.psum(inner(x, y).astype(jnp.bfloat16), "stream") for x, y in pairs]

    lefts = []
    for (x, y), err, fac in zip(pairs, errs, facs):
        tall = exact(fac.T, y, ((1,), (1,)))
        left = exact(tall, x, ((1,), (0,)))
        part = err.shape[0] // streams
        rows = lax.dynamic_slice_in_dim(err, my_stream * part, part, 0)
        mine = lax.dot_general(fac, rows, (((0,), (1,)), ((), ())), precision=HIGH)
        keep = jnp.arange(err.shape[0]) // part == my_stream
        left = left + jnp.where(keep[None], jnp.tile(mine, (1, streams)), 0.0)
        lefts.append(left)
    edges = [0]
    for left in lefts:
        edges.append(edges[-1] + left.shape[1])
    bounds = list(zip(edges[:-1], edges[1:]))
    summed = all_sum(jnp.concatenate(lefts, 1))
    basis = pl.pallas_call(
        lambda *refs: basis_kernel(bounds, *refs),
        out_shape=jax.ShapeDtypeStruct(summed.shape, jnp.float32),
        name="basis",
    )(summed)
    bases = [basis[:, lo:hi] for lo, hi in bounds]

    rights = []
    for (x, y), err, base in zip(pairs, errs, bases):
        tall = exact(base, x, ((1,), (1,)))
        right = exact(tall, y, ((1,), (0,)))
        part = err.shape[0] // streams
        rows = lax.dynamic_slice_in_dim(err, my_stream * part, part, 0)
        share = lax.dynamic_slice_in_dim(base, my_stream * part, part, 1)
        right = right + jnp.dot(share, rows, precision=HIGH)
        rights.append(right)
    edges = [0]
    for right in rights:
        edges.append(edges[-1] + right.shape[1])
    side = -(-packed.shape[0] // 1024) * 128
    packed = jnp.pad(packed, (0, 8 * side - packed.shape[0])).reshape(8, side)
    joined = jnp.concatenate(rights + [packed], 1)
    short = -joined.shape[1] % (128 * devices) if devices <= 32 else -joined.shape[1] % devices
    joined = all_sum(jnp.pad(joined, ((0, 0), (0, short))))
    rights = [joined[:, lo:hi] for lo, hi in zip(edges[:-1], edges[1:])]
    packed_sum = joined[:, edges[-1] : edges[-1] + side].reshape(-1)[: vectors.shape[0]]

    rate = RATE * qdev * math.sqrt(devices / (row + qtok))
    new_w, new_m, new_e = ([], [], [])
    for number in range(5):
        approx = lax.dot_general(
            bases[number], rights[number], (((0,), (0,)), ((), ())), precision=HIGH
        )
        merged = grads[number].astype(jnp.float32) + errs[number]
        new_e.append((merged - approx / replicas)[None])
        momentum = MOMENTUM * moms[number] + approx
        new_m.append(momentum)
        new_w.append(weights[number] - rate * momentum)
    vec_mom = MOMENTUM * mom_vectors + packed_sum
    new_vec = vectors - rate * vec_mom
    return (
        loss,
        *new_w,
        new_vec,
        *new_m,
        vec_mom,
        *new_e,
        *[right.T for right in rights],
    )


def solution(mesh):
    return jax.shard_map(
        shards,
        mesh=mesh,
        in_specs=(
            P(("stream", "replica"), None, None),
            P(("stream", "replica"), None, None),
            P(("stream", "replica"), None),
            P(),
            P(),
            P(),
            P(),
            P(),
            P(),
            P(),
            P(),
            P(),
            P(),
            P(),
            P(),
            P(),
            P(),
            P("replica", None, None),
            P("replica", None, None),
            P("replica", None, None),
            P("replica", None, None),
            P("replica", None, None),
            P(),
            P(),
            P(),
            P(),
            P(),
        ),
        out_specs=(
            P(),
            P(),
            P(),
            P(),
            P(),
            P(),
            P(),
            P(),
            P(),
            P(),
            P(),
            P(),
            P(),
            P("replica", None, None),
            P("replica", None, None),
            P("replica", None, None),
            P("replica", None, None),
            P("replica", None, None),
            P(),
            P(),
            P(),
            P(),
            P(),
        ),
        check_vma=False,
    )
```

```python
import math

import jax
import jax.numpy as jnp
import numpy as np
from jax import lax
from jax.experimental import pallas as pl
from jax.experimental.pallas import tpu as pltpu
from jax.sharding import PartitionSpec as P

D = 384
HEADS = 12
HDIM = 32
FF = 1536
NSEG = 4


HIGH = lax.Precision.HIGHEST
SOFT = 0.03
MOMENTUM = 0.9
RATE = 0.1


def split_vec(packed):
    return jnp.split(
        packed,
        [3 * D, 4 * D, 4 * D + FF, 5 * D + FF, 6 * D + FF, 7 * D + FF, 8 * D + FF, 9 * D + FF],
    )


def inner(first, second):
    return lax.dot_general(
        first, second, (((0,), (0,)), ((), ())), preferred_element_type=jnp.float32
    )


def layer_norm(resid, gain, shift):
    center = resid - jnp.mean(resid, -1, keepdims=True)
    inv_std = lax.rsqrt(jnp.mean(center * center, -1, keepdims=True) + 1e-05)
    normed = center * inv_std
    return (normed * gain + shift, normed, inv_std)


def norm_back(grad_out, gain, normed, inv_std):
    scaled = grad_out * gain
    grad_in = inv_std * (
        scaled
        - jnp.mean(scaled, -1, keepdims=True)
        - normed * jnp.mean(scaled * normed, -1, keepdims=True)
    )
    return (grad_in, jnp.sum(grad_out * normed, 0), jnp.sum(grad_out, 0))


def gelu(value):
    return 0.5 * value * (1.0 + jax.scipy.special.erf(value * 0.7071067811865476))


def gelu_slope(value):
    return (
        0.5 * (1.0 + jax.scipy.special.erf(value * 0.7071067811865476))
        + value * jnp.exp(-0.5 * value * value) * 0.3989422804014327
    )


def rotary(value, cosine, sine):
    half = value.shape[-1] // 2
    return value * cosine + jnp.concatenate([-value[..., half:], value[..., :half]], -1) * sine


def rotary_back(grad, cosine, sine):
    half = grad.shape[-1] // 2
    turned = grad * sine
    return grad * cosine + jnp.concatenate([turned[..., half:], -turned[..., :half]], -1)


def tables(segment):
    count = segment.shape[0]
    places = jnp.arange(count)
    same = segment[:, None] == segment[None, :]
    position = jnp.sum(same & (places[None, :] < places[:, None]), 1).astype(jnp.float32)
    freqs = 10000.0 ** (-(jnp.arange(HDIM // 2).astype(jnp.float32) * 2.0) / HDIM)
    angle = position[:, None] * freqs[None, :]
    cosine = jnp.concatenate([jnp.cos(angle), jnp.cos(angle)], -1)[:, None, :]
    sine = jnp.concatenate([jnp.sin(angle), jnp.sin(angle)], -1)[:, None, :]
    return (same, cosine, sine)


def encode(tokens_in, same, cosine, sine, mats, packed):
    w_qkv, w_out, w_up, w_down, w_head = mats
    b_qkv, b_out, b_up, b_down, gain_one, shift_one, gain_two, shift_two, b_head = split_vec(packed)
    count = tokens_in.shape[0]
    scale = HDIM ** (-0.5)
    qkv = (jnp.dot(tokens_in, w_qkv, preferred_element_type=jnp.float32) + b_qkv).reshape(
        count, 3, HEADS, HDIM
    )
    queries = rotary(qkv[:, 0], cosine, sine).astype(jnp.bfloat16)
    keys_rot = rotary(qkv[:, 1], cosine, sine).astype(jnp.bfloat16)
    values = qkv[:, 2].astype(jnp.bfloat16)
    scores = (
        jnp.einsum("ihd,jhd->hij", queries, keys_rot, preferred_element_type=jnp.float32) * scale
    )
    scores = jnp.where(same[None], scores, -1e30)
    expo = jnp.exp(scores - jnp.max(scores, -1, keepdims=True))
    probs = expo / jnp.sum(expo, -1, keepdims=True)
    probs_low = probs.astype(jnp.bfloat16)
    context = (
        jnp.einsum("hij,jhd->ihd", probs_low, values, preferred_element_type=jnp.float32)
        .reshape(count, D)
        .astype(jnp.bfloat16)
    )
    attended = jnp.dot(context, w_out, preferred_element_type=jnp.float32) + b_out
    hidden_one, normed_one, inv_one = layer_norm(
        tokens_in.astype(jnp.float32) + attended, gain_one, shift_one
    )
    hidden_low = hidden_one.astype(jnp.bfloat16)
    pre_act = jnp.dot(hidden_low, w_up, preferred_element_type=jnp.float32) + b_up
    act_low = gelu(pre_act).astype(jnp.bfloat16)
    mixed = jnp.dot(act_low, w_down, preferred_element_type=jnp.float32) + b_down
    hidden_two, normed_two, inv_two = layer_norm(hidden_one + mixed, gain_two, shift_two)
    second_low = hidden_two.astype(jnp.bfloat16)
    emitted = jnp.dot(second_low, w_head, preferred_element_type=jnp.float32) + b_head
    inv_len = lax.rsqrt(jnp.sum(emitted * emitted, -1, keepdims=True) + 1e-06)
    output = emitted * inv_len
    kept = (
        queries,
        keys_rot,
        values,
        probs,
        probs_low,
        context,
        normed_one,
        inv_one,
        hidden_low,
        pre_act,
        act_low,
        normed_two,
        inv_two,
        second_low,
        inv_len,
        output,
    )
    return (output, kept)


def backward(grad_vec, tokens_in, cosine, sine, kept, mats, packed):
    w_qkv, w_out, w_up, w_down, w_head = mats
    b_qkv, b_out, b_up, b_down, gain_one, shift_one, gain_two, shift_two, b_head = split_vec(packed)
    (
        queries,
        keys_rot,
        values,
        probs,
        probs_low,
        context,
        normed_one,
        inv_one,
        hidden_low,
        pre_act,
        act_low,
        normed_two,
        inv_two,
        second_low,
        inv_len,
        output,
    ) = kept
    count = tokens_in.shape[0]
    scale = HDIM ** (-0.5)
    grad_emit = inv_len * (grad_vec - output * jnp.sum(grad_vec * output, -1, keepdims=True))
    emit_low = grad_emit.astype(jnp.bfloat16)
    grad_hidden_two = jnp.dot(emit_low, w_head.T, preferred_element_type=jnp.float32)
    grad_resid_two, grad_gain_two, grad_shift_two = norm_back(
        grad_hidden_two, gain_two, normed_two, inv_two
    )
    mixed_low = grad_resid_two.astype(jnp.bfloat16)
    grad_act = jnp.dot(mixed_low, w_down.T, preferred_element_type=jnp.float32)
    grad_pre = grad_act * gelu_slope(pre_act)
    pre_low = grad_pre.astype(jnp.bfloat16)
    grad_hidden_one = grad_resid_two + jnp.dot(pre_low, w_up.T, preferred_element_type=jnp.float32)
    grad_resid_one, grad_gain_one, grad_shift_one = norm_back(
        grad_hidden_one, gain_one, normed_one, inv_one
    )
    attn_low = grad_resid_one.astype(jnp.bfloat16)
    grad_context = (
        jnp.dot(attn_low, w_out.T, preferred_element_type=jnp.float32)
        .reshape(count, HEADS, HDIM)
        .astype(jnp.bfloat16)
    )
    grad_probs = jnp.einsum(
        "ihd,jhd->hij", grad_context, values, preferred_element_type=jnp.float32
    )
    grad_values = jnp.einsum(
        "hij,ihd->jhd", probs_low, grad_context, preferred_element_type=jnp.float32
    )
    grad_scores = probs * (grad_probs - jnp.sum(grad_probs * probs, -1, keepdims=True))
    scores_low = grad_scores.astype(jnp.bfloat16)
    grad_queries = (
        jnp.einsum("hij,jhd->ihd", scores_low, keys_rot, preferred_element_type=jnp.float32) * scale
    )
    grad_keys = (
        jnp.einsum("hij,ihd->jhd", scores_low, queries, preferred_element_type=jnp.float32) * scale
    )
    grad_queries = rotary_back(grad_queries, cosine, sine)
    grad_keys = rotary_back(grad_keys, cosine, sine)
    grad_qkv_act = jnp.stack([grad_queries, grad_keys, grad_values], 1).reshape(count, 3 * D)
    grad_packed = jnp.concatenate(
        [
            jnp.sum(grad_qkv_act, 0),
            jnp.sum(grad_resid_one, 0),
            jnp.sum(grad_pre, 0),
            jnp.sum(grad_resid_two, 0),
            grad_gain_one,
            grad_shift_one,
            grad_gain_two,
            grad_shift_two,
            jnp.sum(grad_emit, 0),
        ]
    )
    pairs = (
        (tokens_in, grad_qkv_act.astype(jnp.bfloat16)),
        (context, attn_low),
        (hidden_low, pre_low),
        (act_low, mixed_low),
        (second_low, emit_low),
    )
    return (pairs, grad_packed)


AXES = ("stream", "replica")


def spread(value, devices):
    copies = jnp.broadcast_to(value[None], (devices,) + value.shape)
    return lax.all_to_all(copies, AXES, 0, 0, tiled=True)


def all_sum(value):
    count = lax.axis_size("stream") * lax.axis_size("replica")
    rows, cols = value.shape
    pieces = value.reshape(rows, count, cols // count).transpose(1, 0, 2)
    got = lax.all_to_all(pieces, AXES, 0, 0, tiled=True)
    mine = jnp.sum(got, 0)
    back = spread(mine, count)
    return back.transpose(1, 0, 2).reshape(rows, cols)


def thirds(value):
    high = lax.reduce_precision(value, 8, 7)
    rest = value - high
    mid = lax.reduce_precision(rest, 8, 7)
    low = rest - mid
    return [part.astype(jnp.bfloat16) for part in (high, mid, low)]


def basis_kernel(bounds, left_ref, out_ref):
    blocks = [left_ref[:, lo:hi] for lo, hi in bounds]
    places = lax.broadcasted_iota(jnp.int32, (8, 1), 0)
    for turn in range(8):
        for n, block in enumerate(blocks):
            row = block[turn : turn + 1]
            row = row * lax.rsqrt(jnp.sum(row * row, -1, keepdims=True) + 1e-12)
            shares = jnp.sum(block * row, -1, keepdims=True)
            shares = jnp.where(places > turn, shares, 0.0)
            block = block - shares * row
            blocks[n] = jnp.where(places == turn, row, block)
    for (lo, hi), block in zip(bounds, blocks):
        out_ref[:, lo:hi] = block


def split_rows(value):
    high = value.astype(jnp.bfloat16)
    rest = value - high.astype(jnp.float32)
    mid = rest.astype(jnp.bfloat16)
    low = (rest - mid.astype(jnp.float32)).astype(jnp.bfloat16)
    return [high, mid, low]


def matmul(left, right, contract):
    return lax.dot_general(left, right, (contract, ((), ())), preferred_element_type=jnp.float32)


NN, NT, TN = ((1,), (0,)), ((1,), (1,)), ((0,), (0,))


SPOTS = (0, 3 * D, 4 * D, 4 * D + FF, 5 * D + FF, 6 * D + FF, 7 * D + FF, 8 * D + FF, 9 * D + FF)
SCALE = HDIM ** (-0.5)


def turn_table():
    freqs = (10000.0 ** (-(np.arange(HDIM // 2).astype(np.float32) * 2.0) / HDIM)).astype(np.float32)
    angle = np.arange(256, dtype=np.float32)[:, None] * freqs[None, :]
    wide = np.concatenate([np.tile(np.cos(angle), 8), np.tile(np.sin(angle), 8)], 1)
    rest = wide.astype(np.float32)
    parts = []
    for _ in range(3):
        part = rest.astype(jnp.bfloat16)
        parts.append(part)
        rest = rest - part.astype(np.float32)
    return np.concatenate(parts, 1)


def lanes(shape):
    return lax.broadcasted_iota(jnp.int32, shape, 1)


def turned(value, cosine, sine, sign):
    first = (lanes(value.shape) % HDIM) < HDIM // 2
    if sign > 0:
        rot = jnp.where(first, -pltpu.roll(value, 112, 1), pltpu.roll(value, 16, 1))
        return value * cosine + rot * sine
    part = value * sine
    return value * cosine + jnp.where(first, pltpu.roll(part, 112, 1), -pltpu.roll(part, 16, 1))


def head_mask(head, rows):
    return (lanes((rows, 128)) // HDIM) == head


def bias(vec_ref, n, width):
    return vec_ref[:, SPOTS[n] : SPOTS[n] + width]


def norm(resid):
    center = resid - jnp.mean(resid, -1, keepdims=True)
    inv_std = lax.rsqrt(jnp.mean(center * center, -1, keepdims=True) + 1e-05)
    return center * inv_std, inv_std


def encode_kernel(first, *refs):
    x_ref, pos_ref, segc_ref, segr_ref, table_ref = refs[:5]
    weights, vec_ref = refs[5:10], refs[10]
    (
        q_ref, k_ref, v_ref, ctx_ref, n1_ref, h1_ref, pre_ref, act_ref, n2_ref, h2_ref, out_ref,
        low_ref, stat_ref, cos_ref, sin_ref,
    ) = refs[11:26]
    if first:
        for w_ref, low in zip(weights, refs[26:31]):
            low[...] = w_ref[...].astype(jnp.bfloat16)
        weights = refs[26:31]
    wqkv_ref, wout_ref, wup_ref, wdown_ref, whead_ref = weights
    count = x_ref.shape[0]
    tile = min(count, 128)

    def project(t, _):
        rows = pl.ds(pl.multiple_of(t * tile, tile), tile)
        hot = (pos_ref[rows, :] == lanes((tile, 256))).astype(jnp.bfloat16)
        both = matmul(hot, table_ref[...], NN)
        both = both[:, :256] + both[:, 256:512] + both[:, 512:]
        cosine, sine = both[:, :128], both[:, 128:]
        cos_ref[rows, :] = cosine
        sin_ref[rows, :] = sine
        x = x_ref[rows, :]
        for part, dst in enumerate((q_ref, k_ref, v_ref)):
            val = matmul(x, wqkv_ref[:, part * D : part * D + D], NN) + vec_ref[:, part * D : part * D + D]
            for g in range(3):
                cols = slice(g * 128, g * 128 + 128)
                piece = val[:, cols]
                if part < 2:
                    piece = turned(piece, cosine, sine, 1)
                dst[rows, cols] = piece.astype(jnp.bfloat16)
        return 0

    lax.fori_loop(0, count // tile, project, 0)

    def rest(t, _):
        rows = pl.ds(pl.multiple_of(t * tile, tile), tile)
        same = segc_ref[rows, :] == segr_ref[...]
        stats = jnp.zeros((tile, 128), jnp.float32)
        for g in range(3):
            cols = slice(g * 128, g * 128 + 128)
            q, k, v = q_ref[rows, cols], k_ref[:, cols], v_ref[:, cols]
            total = jnp.zeros((tile, 128), jnp.float32)
            for h in range(4):
                mine = jnp.where(head_mask(h, tile), q, jnp.zeros_like(q))
                scores = matmul(mine, k, NT) * SCALE
                scores = jnp.where(same, scores, -1e30)
                peak = jnp.max(scores, -1, keepdims=True)
                expo = jnp.exp(scores - peak)
                norm_sum = jnp.sum(expo, -1, keepdims=True)
                probs = (expo * (1.0 / norm_sum)).astype(jnp.bfloat16)
                part = matmul(probs, v, NN)
                total = jnp.where(head_mask(h, tile), part, total)
                stats = jnp.where(lanes((tile, 128)) == g * 4 + h, peak + jnp.log(norm_sum), stats)
            ctx_ref[rows, cols] = total.astype(jnp.bfloat16)
        resid = x_ref[rows, :].astype(jnp.float32) + (
            matmul(ctx_ref[rows, :], wout_ref[...], NN) + bias(vec_ref, 1, D)
        )
        normed, inv_one = norm(resid)
        n1_ref[rows, :] = normed
        hidden = normed * bias(vec_ref, 4, D) + bias(vec_ref, 5, D)
        low = hidden.astype(jnp.bfloat16)
        h1_ref[rows, :] = low
        mixed = jnp.zeros((tile, D), jnp.float32)
        for c in range(4):
            cols = slice(c * D, c * D + D)
            pre = matmul(low, wup_ref[:, cols], NN) + vec_ref[:, SPOTS[2] + c * D : SPOTS[2] + c * D + D]
            pre_ref[rows, cols] = pre
            act = gelu(pre).astype(jnp.bfloat16)
            act_ref[rows, cols] = act
            mixed = mixed + matmul(act, wdown_ref[cols, :], NN)
        normed, inv_two = norm(hidden + (mixed + bias(vec_ref, 3, D)))
        n2_ref[rows, :] = normed
        low = (normed * bias(vec_ref, 6, D) + bias(vec_ref, 7, D)).astype(jnp.bfloat16)
        h2_ref[rows, :] = low
        emitted = matmul(low, whead_ref[...], NN) + vec_ref[:, SPOTS[8] : SPOTS[8] + 96]
        inv_len = lax.rsqrt(jnp.sum(emitted * emitted, -1, keepdims=True) + 1e-06)
        out = emitted * inv_len
        out_ref[rows, :] = out
        low_ref[rows, :] = out.astype(jnp.bfloat16)
        place = lanes((tile, 128))
        stats = jnp.where(place == 12, inv_one, stats)
        stats = jnp.where(place == 13, inv_two, stats)
        stat_ref[rows, :] = jnp.where(place == 14, inv_len, stats)
        return 0

    lax.fori_loop(0, count // tile, rest, 0)


def encode_call(tokens, position, segment, table, weights, vectors, first, name):
    count = tokens.shape[0]
    f32, low = jnp.float32, jnp.bfloat16
    shapes = [
        (D, low), (D, low), (D, low), (D, low), (D, f32), (D, low), (FF, f32), (FF, low), (D, f32),
        (D, low), (96, f32), (96, low), (128, f32), (128, f32), (128, f32),
    ]
    outs = [jax.ShapeDtypeStruct((count, width), kind) for width, kind in shapes]
    if first:
        outs += [jax.ShapeDtypeStruct(w.shape, low) for w in weights]
    return pl.pallas_call(
        lambda *refs: encode_kernel(first, *refs), out_shape=outs, name=name
    )(tokens, position[:, None], segment[:, None], segment[None, :], table, *weights, vectors)


def backward_kernel(*refs):
    (
        grad_ref, segc_ref, segr_ref, q_ref, k_ref, v_ref, n1_ref, pre_ref, n2_ref, out_ref,
        stat_ref, cos_ref, sin_ref, wqkv_ref, wout_ref, wup_ref, wdown_ref, whead_ref, vec_ref,
    ) = refs[:19]
    yqkv_ref, yout_ref, yup_ref, ydown_ref, yhead_ref, packed_ref = refs[19:25]
    dk_ref, dv_ref, p_ref, s_ref, c_ref = refs[25:]
    count = q_ref.shape[0]
    tile = min(count, 128)
    packed_ref[...] = jnp.zeros_like(packed_ref)
    dk_ref[...] = jnp.zeros_like(dk_ref)
    dv_ref[...] = jnp.zeros_like(dv_ref)

    def add(n, value, shift=0):
        at = SPOTS[n] + shift
        cols = slice(at, at + value.shape[1])
        packed_ref[:, cols] = packed_ref[:, cols] + jnp.sum(value, 0, keepdims=True)

    def norm_grad(grad, gain, normed, inv_std):
        scaled = grad * gain
        return inv_std * (
            scaled
            - jnp.mean(scaled, -1, keepdims=True)
            - normed * jnp.mean(scaled * normed, -1, keepdims=True)
        )

    def step(t, _):
        rows = pl.ds(pl.multiple_of(t * tile, tile), tile)
        stats = stat_ref[rows, :]
        grad_vec = grad_ref[rows, :] if len(grad_ref.shape) == 2 else jnp.sum(grad_ref[...], 0)
        output = out_ref[rows, :]
        emit = stats[:, 14:15] * (grad_vec - output * jnp.sum(grad_vec * output, -1, keepdims=True))
        add(8, emit)
        low = emit.astype(jnp.bfloat16)
        yhead_ref[rows, :] = low
        grad = matmul(low, whead_ref[...], NT)
        normed = n2_ref[rows, :]
        resid_two = norm_grad(grad, bias(vec_ref, 6, D), normed, stats[:, 13:14])
        add(6, grad * normed)
        add(7, grad)
        add(3, resid_two)
        low = resid_two.astype(jnp.bfloat16)
        ydown_ref[rows, :] = low
        grad = resid_two
        for c in range(4):
            cols = slice(c * D, c * D + D)
            pre = matmul(low, wdown_ref[cols, :], NT) * gelu_slope(pre_ref[rows, cols])
            add(2, pre, c * D)
            pre = pre.astype(jnp.bfloat16)
            yup_ref[rows, cols] = pre
            grad = grad + matmul(pre, wup_ref[:, cols], NT)
        normed = n1_ref[rows, :]
        resid_one = norm_grad(grad, bias(vec_ref, 4, D), normed, stats[:, 12:13])
        add(4, grad * normed)
        add(5, grad)
        add(1, resid_one)
        low = resid_one.astype(jnp.bfloat16)
        yout_ref[rows, :] = low
        grad_ctx = matmul(low, wout_ref[...], NT).astype(jnp.bfloat16)
        same = segc_ref[rows, :] == segr_ref[...]
        cosine, sine = cos_ref[rows, :], sin_ref[rows, :]
        for g in range(3):
            cols = slice(g * 128, g * 128 + 128)
            q, k, v = q_ref[rows, cols], k_ref[:, cols], v_ref[:, cols]
            dctx = grad_ctx[:, cols]
            dq = jnp.zeros((tile, 128), jnp.float32)
            for h in range(4):
                mask = head_mask(h, tile)
                mine = jnp.where(mask, q, jnp.zeros_like(q))
                back = jnp.where(mask, dctx, jnp.zeros_like(dctx))
                place = slice(h * tile, h * tile + tile)
                scores = matmul(mine, k, NT) * SCALE
                head = g * 4 + h
                probs = jnp.where(same, jnp.exp(scores - stats[:, head : head + 1]), 0.0)
                gprob = matmul(back, v, NT)
                weighed = gprob * probs
                gscore = weighed - probs * jnp.sum(weighed, -1, keepdims=True)
                gscore = gscore.astype(jnp.bfloat16)
                p_ref[place, :] = probs.astype(jnp.bfloat16)
                s_ref[place, :] = gscore
                c_ref[place, :] = back
                c_ref[4 * tile + h * tile : 4 * tile + h * tile + tile, :] = mine
                dq = jnp.where(mask, matmul(gscore, k, NN), dq)
            dv_ref[:, cols] = dv_ref[:, cols] + matmul(p_ref[...], c_ref[: 4 * tile, :], TN)
            dk_ref[:, cols] = dk_ref[:, cols] + matmul(s_ref[...], c_ref[4 * tile :, :], TN)
            dq = turned(dq * SCALE, cosine, sine, -1)
            add(0, dq, g * 128)
            yqkv_ref[rows, cols] = dq.astype(jnp.bfloat16)
        return 0

    lax.fori_loop(0, count // tile, step, 0)

    def last(t, _):
        rows = pl.ds(pl.multiple_of(t * tile, tile), tile)
        cosine, sine = cos_ref[rows, :], sin_ref[rows, :]
        for g in range(3):
            cols = slice(g * 128, g * 128 + 128)
            dk = turned(dk_ref[rows, cols] * SCALE, cosine, sine, -1)
            dv = dv_ref[rows, cols]
            add(0, dk, D + g * 128)
            add(0, dv, 2 * D + g * 128)
            yqkv_ref[rows, D + g * 128 : D + g * 128 + 128] = dk.astype(jnp.bfloat16)
            yqkv_ref[rows, 2 * D + g * 128 : 2 * D + g * 128 + 128] = dv.astype(jnp.bfloat16)
        return 0

    lax.fori_loop(0, count // tile, last, 0)


def backward_call(grad, segment, kept, weights, vectors, name):
    q, k, v, _, n1, _, pre, _, n2, _, out, _, stat, cosine, sine = kept
    count = q.shape[0]
    tile = min(count, 128)
    f32, low = jnp.float32, jnp.bfloat16
    outs = [jax.ShapeDtypeStruct((count, width), low) for width in (3 * D, D, FF, D, 96)]
    return pl.pallas_call(
        backward_kernel,
        out_shape=outs + [jax.ShapeDtypeStruct((1, 5120), f32)],
        scratch_shapes=[
            pltpu.VMEM((count, D), f32),
            pltpu.VMEM((count, D), f32),
            pltpu.VMEM((4 * tile, count), low),
            pltpu.VMEM((4 * tile, count), low),
            pltpu.VMEM((8 * tile, 128), low),
        ],
        name=name,
    )(
        grad, segment[:, None], segment[None, :], q, k, v, n1, pre, n2, out, stat, cosine, sine,
        *weights, vectors,
    )


def early_kernel(me_ref, *refs):
    fac_refs, err_refs, early_ref, parts_ref = refs[:5], refs[5:10], refs[10], refs[11]
    eye = (
        lax.broadcasted_iota(jnp.int32, (8, 8), 0) == lax.broadcasted_iota(jnp.int32, (8, 8), 1)
    ).astype(jnp.bfloat16)
    at = to = 0
    for fac_ref, err_ref in zip(fac_refs, err_refs):
        quarter, wide = err_ref.shape
        parts = [matmul(eye, part, NT) for part in split_rows(fac_ref[...])]
        parts = jnp.concatenate(parts, 0).astype(jnp.bfloat16)
        parts_ref[:, to : to + wide] = parts
        to += wide
        total = jnp.zeros((24, quarter), jnp.float32)
        for part in split_rows(err_ref[...]):
            total = total + matmul(parts, part, NT)
        total = total[:8] + total[8:16] + total[16:24]
        spread_out = jnp.concatenate([total] * 4, 1)
        spot = lanes(spread_out.shape) // quarter
        early_ref[:, at : at + 4 * quarter] = jnp.where(spot == me_ref[0], spread_out, 0.0)
        at += 4 * quarter


def grads_kernel(me_ref, *refs):
    acts, parts_ref, early_ref, packed_refs = refs[:20], refs[20], refs[21], refs[22:24]
    a_ref, b_ref, left_ref = refs[24:]
    me = me_ref[0]

    def turns(quarter):
        turn = quarter ^ me
        return (turn & 1) * 2 + (turn >> 1), turn

    def place(block, value):
        low = value.astype(jnp.bfloat16)
        for quarter in range(4):
            a_at, b_at = turns(quarter)
            rows = low[quarter * 96 : quarter * 96 + 96]
            if block < 6:
                a_ref[a_at, block * 96 : block * 96 + 96, :] = rows
            elif block < 12:
                b_ref[b_at, (block - 6) * 96 : (block - 6) * 96 + 96, :] = rows
            else:
                for part in range(3):
                    b_ref[b_at, 576:608, part * 128 : part * 128 + 96] = rows[
                        part * 32 : part * 32 + 32
                    ]
                    b_ref[b_at, 576:608, part * 128 + 96 : part * 128 + 128] = jnp.zeros(
                        (32, 32), jnp.bfloat16
                    )

    block = at = to = 0
    for n in range(5):
        dx_ref, qx_ref, dy_ref, qy_ref = acts[4 * n : 4 * n + 4]
        parts = parts_ref[:, to : to + dy_ref.shape[1]]
        to += dy_ref.shape[1]
        tall_d = matmul(dy_ref[...], parts, NT)
        tall_q = matmul(qy_ref[...], parts, NT)
        parts = []
        for tall in (tall_d, tall_q):
            tall = tall[:, :8] + tall[:, 8:16] + tall[:, 16:24]
            parts.append(jnp.concatenate(split_rows(tall), 1))
        wide = dx_ref.shape[1]
        left = matmul(parts[0], dx_ref[...], TN) + matmul(parts[1], qx_ref[...], TN)
        left_ref[:, at : at + wide] = (
            left[:8] + left[8:16] + left[16:24] + early_ref[:, at : at + wide]
        )
        at += wide
        for k in range(wide // 384):
            for c in range(-(-dy_ref.shape[1] // 384)):
                rows, cols = slice(k * 384, k * 384 + 384), slice(c * 384, c * 384 + 384)
                place(
                    block,
                    matmul(dx_ref[:, rows], dy_ref[:, cols], TN)
                    + matmul(qx_ref[:, rows], qy_ref[:, cols], TN),
                )
                block += 1
    side = packed_refs[0].shape[1] // 8
    for r in range(8):
        cols = slice(r * side, r * side + side)
        left_ref[r : r + 1, at : at + side] = packed_refs[0][:, cols] + packed_refs[1][:, cols]
    left_ref[:, at + side :] = jnp.zeros((8, left_ref.shape[1] - at - side), jnp.float32)


def factors_kernel(bounds, me_ref, left_ref, *refs):
    acts, err_refs = refs[:20], refs[20:25]
    basis_ref, right_ref = refs[25:]
    me = me_ref[0]
    basis_kernel(bounds, left_ref, basis_ref)
    at = 0
    for n, (lo, hi) in enumerate(bounds):
        dx_ref, qx_ref, dy_ref, qy_ref = acts[4 * n : 4 * n + 4]
        base = basis_ref[:, lo:hi]
        base_parts = jnp.concatenate(split_rows(base), 0)
        total = None
        for x_ref, y_ref in ((dx_ref, dy_ref), (qx_ref, qy_ref)):
            tall = matmul(x_ref[...], base_parts, NT)
            tall = tall[:, :8] + tall[:, 8:16] + tall[:, 16:24]
            right = matmul(jnp.concatenate(split_rows(tall), 1), y_ref[...], TN)
            total = right if total is None else total + right
        quarter = (hi - lo) // 4
        share = jnp.zeros((8, quarter), jnp.float32)
        for k in range(4):
            share = jnp.where(me == k, base[:, k * quarter : (k + 1) * quarter], share)
        share = jnp.concatenate(split_rows(share), 0)
        for part in split_rows(err_refs[n][...]):
            total = total + matmul(share, part, NN)
        wide = dy_ref.shape[1]
        right_ref[:, at : at + wide] = total[:8] + total[8:16] + total[16:24]
        at += wide
    right_ref[:, at:] = jnp.zeros((8, right_ref.shape[1] - at), jnp.float32)


def weight_kernel(spans, rate, *refs):
    right_ref = refs[0]
    for n, (at, span) in enumerate(spans):
        basis_ref, mom_ref, w_ref = refs[1 + 3 * n : 4 + 3 * n]
        new_w_ref, new_m_ref = refs[1 + 3 * len(spans) + 2 * n : 3 + 3 * len(spans) + 2 * n]
        approx = matmul(basis_ref[...], right_ref[:, at : at + span], NN)
        moved = MOMENTUM * mom_ref[...] + approx
        new_m_ref[...] = moved
        new_w_ref[...] = w_ref[...] - rate * moved


def error_kernel(spans, replicas, me_ref, right_ref, a_ref, b_ref, *refs):
    basis_refs, err_refs, new_refs = refs[:5], refs[5:10], refs[10:]
    share = 1.0 / replicas

    def grad(block):
        if block < 6:
            return a_ref[0, block * 96 : block * 96 + 96, :]
        return b_ref[0, (block - 6) * 96 : (block - 6) * 96 + 96, :]

    block = 0
    for n, (at, span) in enumerate(spans):
        if n == 3:
            for k in range(4):
                approx = matmul(basis_refs[n][k], right_ref[:, at : at + span], NN)
                merged = grad(block).astype(jnp.float32) + err_refs[n][k]
                new_refs[n][k] = merged - approx * share
                block += 1
            continue
        approx = matmul(basis_refs[n][...], right_ref[:, at : at + span], NN)
        if n == 4:
            for part in range(3):
                rows = slice(part * 32, part * 32 + 32)
                piece = b_ref[0, 576:608, part * 128 : part * 128 + 96]
                new_refs[n][rows] = (
                    piece.astype(jnp.float32) + err_refs[n][rows] - approx[rows] * share
                )
            continue
        for c in range(span // 384):
            cols = slice(c * 384, c * 384 + 384)
            merged = grad(block).astype(jnp.float32) + err_refs[n][:, cols]
            new_refs[n][:, cols] = merged - approx[:, cols] * share
            block += 1


def whole(value):
    return pl.BlockSpec(value.shape, lambda i, me: (0,) * value.ndim)


def exchange(value, turn):
    return lax.ppermute(value, "stream", [(i, i ^ turn) for i in range(4)])


def stream_sum(a, b):
    def add(first, second):
        return (first.astype(jnp.float32) + second.astype(jnp.float32)).astype(jnp.bfloat16)

    both = []
    got = [exchange(a[2:], 1), exchange(b[2:], 2)]
    half = [add(a[:2], got[0]), add(b[:2], got[1])]
    got = [exchange(half[0][1], 2), exchange(half[1][1], 1)]
    full = [add(half[0][0], got[0]), add(half[1][0], got[1])]
    got = [exchange(full[0], 2), exchange(full[1], 1)]
    pair = [jnp.stack([one, two], 0) for one, two in zip(full, got)]
    last = [exchange(pair[0], 1), exchange(pair[1], 2)]
    return [jnp.concatenate([one, two], 0) for one, two in zip(pair, last)]


def blocked(kernel, right, operands, outs, steps, name):
    spec = [
        pl.BlockSpec((v.shape[0] // steps, v.shape[1]), lambda i: (i, 0)) for v in operands + outs
    ]
    return pl.pallas_call(
        kernel,
        grid=(steps,),
        in_specs=[pl.BlockSpec(right.shape, lambda i: (0, 0))] + spec[: len(operands)],
        out_specs=spec[len(operands) :],
        out_shape=outs,
        name=name,
    )(right, *operands)


def shards(
    query_embeds,
    doc_embeds,
    doc_segments,
    candidates,
    neg_counts,
    w_qkv,
    w_out,
    w_up,
    w_down,
    w_head,
    vectors,
    mom_qkv,
    mom_out,
    mom_up,
    mom_down,
    mom_head,
    mom_vectors,
    err_qkv,
    err_out,
    err_up,
    err_down,
    err_head,
    fac_qkv,
    fac_out,
    fac_up,
    fac_down,
    fac_head,
):
    streams, replicas = lax.axis_size("stream"), lax.axis_size("replica")
    devices = streams * replicas
    my_stream, me = lax.axis_index("stream"), lax.axis_index(AXES)
    qdev, qlen, width = query_embeds.shape
    row = doc_embeds.shape[1]
    qtok = qdev * qlen
    weights = (w_qkv, w_out, w_up, w_down, w_head)
    moms = (mom_qkv, mom_out, mom_up, mom_down, mom_head)
    errs = (err_qkv[0], err_out[0], err_up[0], err_down[0], err_head[0])
    facs = (fac_qkv, fac_out, fac_up, fac_down, fac_head)
    vec_row = vectors[None, :]
    table = jnp.asarray(turn_table())
    query_in = query_embeds.reshape(qtok, width)
    query_seg = jnp.arange(qtok, dtype=jnp.int32) // qlen
    *query_kept, m0, m1, m2, m3, m4 = encode_call(
        query_in, jnp.arange(qtok, dtype=jnp.int32) % qlen, query_seg, table, weights, vec_row,
        True, "encode_queries",
    )
    mats = (m0, m1, m2, m3, m4)
    all_query = spread(query_kept[11], devices)

    doc_in = doc_embeds[0]
    doc_seg = doc_segments[0]
    starts = jnp.sum(doc_seg[None, :] < jnp.arange(NSEG)[:, None], 1)
    begin = sum(jnp.where(doc_seg == d, starts[d], 0) for d in range(NSEG))
    doc_pos = jnp.arange(row, dtype=jnp.int32) - begin
    doc_kept = encode_call(
        doc_in, doc_pos, doc_seg, table, mats, vec_row, False, "encode_documents"
    )
    doc_low = doc_kept[11]
    pdim = doc_low.shape[1]

    tokens = devices * qtok
    rows_all = all_query.reshape(tokens, pdim)
    segment = doc_segments[0]
    sims = (
        lax.dot_general(
            doc_low, rows_all, (((1,), (1,)), ((), ())), preferred_element_type=jnp.float32
        )
        / SOFT
    )
    weight = jnp.exp(sims)
    segmask = (segment[None, :] == jnp.arange(NSEG)[:, None]).astype(jnp.float32)
    totals = jnp.stack(
        [jnp.sum(jnp.where((segment == d)[:, None], weight, 0.0), 0) for d in range(NSEG)], 0
    )
    scores = (SOFT * jnp.log(totals)).reshape(NSEG, devices, qdev, qlen).sum(-1)
    scores = scores.reshape(NSEG, devices * qdev)
    table = spread(scores, devices).reshape(devices * NSEG, devices * qdev)
    me_stream = my_stream[None].astype(jnp.int32)
    height, wide = sum(w.shape[0] for w in weights), sum(w.shape[1] for w in weights)
    early, fac_parts = pl.pallas_call(
        early_kernel,
        grid_spec=pltpu.PrefetchScalarGridSpec(
            num_scalar_prefetch=1,
            grid=(1,),
            in_specs=[whole(v) for v in facs]
            + [
                pl.BlockSpec((e.shape[0] // 4, e.shape[1]), lambda i, me: (me[0], 0))
                for e in errs
            ],
            out_specs=[
                pl.BlockSpec((8, height), lambda i, me: (0, 0)),
                pl.BlockSpec((24, wide), lambda i, me: (0, 0)),
            ],
        ),
        out_shape=[
            jax.ShapeDtypeStruct((8, height), jnp.float32),
            jax.ShapeDtypeStruct((24, wide), jnp.bfloat16),
        ],
        name="early",
    )(me_stream, *facs, *lax.optimization_barrier((errs, scores))[0])
    docs = jnp.arange(devices * NSEG)
    slots = jnp.arange(candidates.shape[1])
    named = (candidates[None] == docs[:, None, None]) & (slots <= neg_counts[:, None])[None]
    first = (candidates[:, 0][None] == docs[:, None]).astype(jnp.float32)
    listed = jnp.any(named, -1)
    logits = jnp.where(listed, table, -1e30)
    peak = jnp.max(logits, 0, keepdims=True)
    expo = jnp.exp(logits - peak)
    total = jnp.sum(expo, 0, keepdims=True)
    total_queries = candidates.shape[0]
    losses = peak[0] + jnp.log(total[0]) - jnp.sum(table * first, 0)
    loss = jnp.mean(losses)
    grad_table = (expo / total - first) / total_queries
    own = lax.dynamic_slice_in_dim(grad_table, me * NSEG, NSEG, 0)
    per_token = jnp.repeat(own, qlen, axis=1) / totals
    spots = jnp.sum(segmask[:, :, None] * per_token[:, None, :], 0)
    sim_low = (weight * spots).astype(jnp.bfloat16)
    query_grad = lax.dot_general(
        sim_low, doc_low, (((0,), (0,)), ((), ())), preferred_element_type=jnp.float32
    ).reshape(devices, qtok, pdim)
    query_local = lax.all_to_all(query_grad, AXES, 0, 0, tiled=True)
    doc_grad = jnp.dot(sim_low, rows_all, preferred_element_type=jnp.float32)

    *doc_out, doc_packed = backward_call(
        doc_grad, doc_seg, doc_kept, mats, vec_row, "backward_documents"
    )
    *query_out, query_packed = backward_call(
        query_local, query_seg, query_kept, mats, vec_row, "backward_queries"
    )
    inputs = ((doc_in, query_in),) + tuple((doc_kept[n], query_kept[n]) for n in (3, 5, 7, 9))
    acts = [
        v for (dx, qx), dy, qy in zip(inputs, doc_out, query_out) for v in (dx, qx, dy, qy)
    ]
    edges = [0]
    for w in weights:
        edges.append(edges[-1] + w.shape[0])
    bounds = list(zip(edges[:-1], edges[1:]))
    side = doc_packed.shape[1] // 8
    full = edges[-1] + side
    full += -full % (128 * devices) if devices <= 32 else -full % (16 * devices)
    a_grads, b_grads, left = pl.pallas_call(
        grads_kernel,
        grid_spec=pltpu.PrefetchScalarGridSpec(
            num_scalar_prefetch=1,
            grid=(1,),
            in_specs=[whole(v) for v in acts + [fac_parts, early, doc_packed, query_packed]],
            out_specs=[
                pl.BlockSpec((4, 576, D), lambda i, me: (0, 0, 0)),
                pl.BlockSpec((4, 608, D), lambda i, me: (0, 0, 0)),
                pl.BlockSpec((8, full), lambda i, me: (0, 0)),
            ],
        ),
        out_shape=[
            jax.ShapeDtypeStruct((4, 576, D), jnp.bfloat16),
            jax.ShapeDtypeStruct((4, 608, D), jnp.bfloat16),
            jax.ShapeDtypeStruct((8, full), jnp.float32),
        ],
        name="grads",
    )(me_stream, *acts, fac_parts, early, doc_packed, query_packed)
    a_sums, b_sums = stream_sum(a_grads, b_grads)

    summed = all_sum(left)
    packed_sum = summed[:, edges[-1] : edges[-1] + side].reshape(-1)[: vectors.shape[0]]

    wide = sum(w.shape[1] for w in weights)
    wide += -wide % (128 * devices) if devices <= 32 else -wide % (128 * devices // 8)
    basis, right = pl.pallas_call(
        lambda *refs: factors_kernel(bounds, *refs),
        grid_spec=pltpu.PrefetchScalarGridSpec(
            num_scalar_prefetch=1,
            grid=(1,),
            in_specs=[whole(summed)]
            + [whole(v) for v in acts]
            + [
                pl.BlockSpec((e.shape[0] // 4, e.shape[1]), lambda i, me: (me[0], 0))
                for e in errs
            ],
            out_specs=[
                pl.BlockSpec((8, edges[-1]), lambda i, me: (0, 0)),
                pl.BlockSpec((8, wide), lambda i, me: (0, 0)),
            ],
        ),
        out_shape=[
            jax.ShapeDtypeStruct((8, edges[-1]), jnp.float32),
            jax.ShapeDtypeStruct((8, wide), jnp.float32),
        ],
        name="factors",
    )(me_stream, summed, *acts, *errs)
    joined = all_sum(right)
    rights, spans, at = [], [], 0
    for w in weights:
        rights.append(joined[:, at : at + w.shape[1]])
        spans.append((at, w.shape[1]))
        at += w.shape[1]

    rate = RATE * qdev * math.sqrt(devices / (row + qtok))
    firsts, seconds = thirds(basis), thirds(joined)
    left_parts = jnp.concatenate([firsts[k] for k in (0, 0, 1, 0, 1, 2)], 0).T
    right_parts = jnp.concatenate([seconds[k] for k in (0, 1, 0, 2, 1, 0)], 0)
    left_parts = [left_parts[lo:hi] for lo, hi in bounds]
    out = [jax.ShapeDtypeStruct(w.shape, jnp.float32) for w in weights]
    moved = blocked(
        lambda *refs: weight_kernel(spans, rate, *refs),
        right_parts,
        [v for trio in zip(left_parts, moms, weights) for v in trio],
        [v for v in out for _ in range(2)],
        6,
        "weights",
    )
    new_w, new_m = moved[0::2], moved[1::2]

    def quartered(value):
        if value.shape[0] == 4 * D:
            return value.reshape(4, D, value.shape[1])
        return value

    def quarter_spec(value):
        if len(value.shape) == 3:
            return pl.BlockSpec((4, D // 4, value.shape[2]), lambda q, me: (0, q, 0))
        return pl.BlockSpec((D // 4, value.shape[1]), lambda q, me: (q, 0))

    rows = [quartered(v) for v in left_parts] + [quartered(v) for v in errs]
    out = [jax.ShapeDtypeStruct(quartered(e).shape, jnp.float32) for e in errs]
    new_e = pl.pallas_call(
        lambda *refs: error_kernel(spans, replicas, *refs),
        grid_spec=pltpu.PrefetchScalarGridSpec(
            num_scalar_prefetch=1,
            grid=(4,),
            in_specs=[
                pl.BlockSpec(right_parts.shape, lambda q, me: (0, 0)),
                pl.BlockSpec(
                    (1, 576, D), lambda q, me: (((q ^ me[0]) & 1) * 2 + ((q ^ me[0]) >> 1), 0, 0)
                ),
                pl.BlockSpec((1, 608, D), lambda q, me: (q ^ me[0], 0, 0)),
            ]
            + [quarter_spec(v) for v in rows],
            out_specs=[quarter_spec(v) for v in out],
        ),
        out_shape=out,
        name="errors",
    )(me_stream, right_parts, a_sums, b_sums, *rows)
    new_e = [v.reshape((1,) + e.shape) for v, e in zip(new_e, errs)]
    vec_mom = MOMENTUM * mom_vectors + packed_sum
    new_vec = vectors - rate * vec_mom
    return (
        loss,
        *new_w,
        new_vec,
        *new_m,
        vec_mom,
        *new_e,
        *[right.T for right in rights],
    )


def solution(mesh):
    return jax.shard_map(
        shards,
        mesh=mesh,
        in_specs=(
            P(("stream", "replica"), None, None),
            P(("stream", "replica"), None, None),
            P(("stream", "replica"), None),
            P(),
            P(),
            P(),
            P(),
            P(),
            P(),
            P(),
            P(),
            P(),
            P(),
            P(),
            P(),
            P(),
            P(),
            P("replica", None, None),
            P("replica", None, None),
            P("replica", None, None),
            P("replica", None, None),
            P("replica", None, None),
            P(),
            P(),
            P(),
            P(),
            P(),
        ),
        out_specs=(
            P(),
            P(),
            P(),
            P(),
            P(),
            P(),
            P(),
            P(),
            P(),
            P(),
            P(),
            P(),
            P(),
            P("replica", None, None),
            P("replica", None, None),
            P("replica", None, None),
            P("replica", None, None),
            P("replica", None, None),
            P(),
            P(),
            P(),
            P(),
            P(),
        ),
        check_vma=False,
    )
```

```python
import math

import jax
import jax.numpy as jnp
import numpy as np
from jax import lax
from jax.experimental import pallas as pl
from jax.experimental.pallas import tpu as pltpu
from jax.sharding import PartitionSpec as P

D = 384
HEADS = 12
HDIM = 32
FF = 1536
NSEG = 4


HIGH = lax.Precision.HIGHEST
SOFT = 0.03
MOMENTUM = 0.9
RATE = 0.1


def split_vec(packed):
    return jnp.split(
        packed,
        [3 * D, 4 * D, 4 * D + FF, 5 * D + FF, 6 * D + FF, 7 * D + FF, 8 * D + FF, 9 * D + FF],
    )


def inner(first, second):
    return lax.dot_general(
        first, second, (((0,), (0,)), ((), ())), preferred_element_type=jnp.float32
    )


def layer_norm(resid, gain, shift):
    center = resid - jnp.mean(resid, -1, keepdims=True)
    inv_std = lax.rsqrt(jnp.mean(center * center, -1, keepdims=True) + 1e-05)
    normed = center * inv_std
    return (normed * gain + shift, normed, inv_std)


def norm_back(grad_out, gain, normed, inv_std):
    scaled = grad_out * gain
    grad_in = inv_std * (
        scaled
        - jnp.mean(scaled, -1, keepdims=True)
        - normed * jnp.mean(scaled * normed, -1, keepdims=True)
    )
    return (grad_in, jnp.sum(grad_out * normed, 0), jnp.sum(grad_out, 0))


def gelu(value):
    return 0.5 * value * (1.0 + jax.scipy.special.erf(value * 0.7071067811865476))


def gelu_slope(value):
    return (
        0.5 * (1.0 + jax.scipy.special.erf(value * 0.7071067811865476))
        + value * jnp.exp(-0.5 * value * value) * 0.3989422804014327
    )


def rotary(value, cosine, sine):
    half = value.shape[-1] // 2
    return value * cosine + jnp.concatenate([-value[..., half:], value[..., :half]], -1) * sine


def rotary_back(grad, cosine, sine):
    half = grad.shape[-1] // 2
    turned = grad * sine
    return grad * cosine + jnp.concatenate([turned[..., half:], -turned[..., :half]], -1)


def tables(segment):
    count = segment.shape[0]
    places = jnp.arange(count)
    same = segment[:, None] == segment[None, :]
    position = jnp.sum(same & (places[None, :] < places[:, None]), 1).astype(jnp.float32)
    freqs = 10000.0 ** (-(jnp.arange(HDIM // 2).astype(jnp.float32) * 2.0) / HDIM)
    angle = position[:, None] * freqs[None, :]
    cosine = jnp.concatenate([jnp.cos(angle), jnp.cos(angle)], -1)[:, None, :]
    sine = jnp.concatenate([jnp.sin(angle), jnp.sin(angle)], -1)[:, None, :]
    return (same, cosine, sine)


def encode(tokens_in, same, cosine, sine, mats, packed):
    w_qkv, w_out, w_up, w_down, w_head = mats
    b_qkv, b_out, b_up, b_down, gain_one, shift_one, gain_two, shift_two, b_head = split_vec(packed)
    count = tokens_in.shape[0]
    scale = HDIM ** (-0.5)
    qkv = (jnp.dot(tokens_in, w_qkv, preferred_element_type=jnp.float32) + b_qkv).reshape(
        count, 3, HEADS, HDIM
    )
    queries = rotary(qkv[:, 0], cosine, sine).astype(jnp.bfloat16)
    keys_rot = rotary(qkv[:, 1], cosine, sine).astype(jnp.bfloat16)
    values = qkv[:, 2].astype(jnp.bfloat16)
    scores = (
        jnp.einsum("ihd,jhd->hij", queries, keys_rot, preferred_element_type=jnp.float32) * scale
    )
    scores = jnp.where(same[None], scores, -1e30)
    expo = jnp.exp(scores - jnp.max(scores, -1, keepdims=True))
    probs = expo / jnp.sum(expo, -1, keepdims=True)
    probs_low = probs.astype(jnp.bfloat16)
    context = (
        jnp.einsum("hij,jhd->ihd", probs_low, values, preferred_element_type=jnp.float32)
        .reshape(count, D)
        .astype(jnp.bfloat16)
    )
    attended = jnp.dot(context, w_out, preferred_element_type=jnp.float32) + b_out
    hidden_one, normed_one, inv_one = layer_norm(
        tokens_in.astype(jnp.float32) + attended, gain_one, shift_one
    )
    hidden_low = hidden_one.astype(jnp.bfloat16)
    pre_act = jnp.dot(hidden_low, w_up, preferred_element_type=jnp.float32) + b_up
    act_low = gelu(pre_act).astype(jnp.bfloat16)
    mixed = jnp.dot(act_low, w_down, preferred_element_type=jnp.float32) + b_down
    hidden_two, normed_two, inv_two = layer_norm(hidden_one + mixed, gain_two, shift_two)
    second_low = hidden_two.astype(jnp.bfloat16)
    emitted = jnp.dot(second_low, w_head, preferred_element_type=jnp.float32) + b_head
    inv_len = lax.rsqrt(jnp.sum(emitted * emitted, -1, keepdims=True) + 1e-06)
    output = emitted * inv_len
    kept = (
        queries,
        keys_rot,
        values,
        probs,
        probs_low,
        context,
        normed_one,
        inv_one,
        hidden_low,
        pre_act,
        act_low,
        normed_two,
        inv_two,
        second_low,
        inv_len,
        output,
    )
    return (output, kept)


def backward(grad_vec, tokens_in, cosine, sine, kept, mats, packed):
    w_qkv, w_out, w_up, w_down, w_head = mats
    b_qkv, b_out, b_up, b_down, gain_one, shift_one, gain_two, shift_two, b_head = split_vec(packed)
    (
        queries,
        keys_rot,
        values,
        probs,
        probs_low,
        context,
        normed_one,
        inv_one,
        hidden_low,
        pre_act,
        act_low,
        normed_two,
        inv_two,
        second_low,
        inv_len,
        output,
    ) = kept
    count = tokens_in.shape[0]
    scale = HDIM ** (-0.5)
    grad_emit = inv_len * (grad_vec - output * jnp.sum(grad_vec * output, -1, keepdims=True))
    emit_low = grad_emit.astype(jnp.bfloat16)
    grad_hidden_two = jnp.dot(emit_low, w_head.T, preferred_element_type=jnp.float32)
    grad_resid_two, grad_gain_two, grad_shift_two = norm_back(
        grad_hidden_two, gain_two, normed_two, inv_two
    )
    mixed_low = grad_resid_two.astype(jnp.bfloat16)
    grad_act = jnp.dot(mixed_low, w_down.T, preferred_element_type=jnp.float32)
    grad_pre = grad_act * gelu_slope(pre_act)
    pre_low = grad_pre.astype(jnp.bfloat16)
    grad_hidden_one = grad_resid_two + jnp.dot(pre_low, w_up.T, preferred_element_type=jnp.float32)
    grad_resid_one, grad_gain_one, grad_shift_one = norm_back(
        grad_hidden_one, gain_one, normed_one, inv_one
    )
    attn_low = grad_resid_one.astype(jnp.bfloat16)
    grad_context = (
        jnp.dot(attn_low, w_out.T, preferred_element_type=jnp.float32)
        .reshape(count, HEADS, HDIM)
        .astype(jnp.bfloat16)
    )
    grad_probs = jnp.einsum(
        "ihd,jhd->hij", grad_context, values, preferred_element_type=jnp.float32
    )
    grad_values = jnp.einsum(
        "hij,ihd->jhd", probs_low, grad_context, preferred_element_type=jnp.float32
    )
    grad_scores = probs * (grad_probs - jnp.sum(grad_probs * probs, -1, keepdims=True))
    scores_low = grad_scores.astype(jnp.bfloat16)
    grad_queries = (
        jnp.einsum("hij,jhd->ihd", scores_low, keys_rot, preferred_element_type=jnp.float32) * scale
    )
    grad_keys = (
        jnp.einsum("hij,ihd->jhd", scores_low, queries, preferred_element_type=jnp.float32) * scale
    )
    grad_queries = rotary_back(grad_queries, cosine, sine)
    grad_keys = rotary_back(grad_keys, cosine, sine)
    grad_qkv_act = jnp.stack([grad_queries, grad_keys, grad_values], 1).reshape(count, 3 * D)
    grad_packed = jnp.concatenate(
        [
            jnp.sum(grad_qkv_act, 0),
            jnp.sum(grad_resid_one, 0),
            jnp.sum(grad_pre, 0),
            jnp.sum(grad_resid_two, 0),
            grad_gain_one,
            grad_shift_one,
            grad_gain_two,
            grad_shift_two,
            jnp.sum(grad_emit, 0),
        ]
    )
    pairs = (
        (tokens_in, grad_qkv_act.astype(jnp.bfloat16)),
        (context, attn_low),
        (hidden_low, pre_low),
        (act_low, mixed_low),
        (second_low, emit_low),
    )
    return (pairs, grad_packed)


AXES = ("stream", "replica")


def spread(value, devices):
    copies = jnp.broadcast_to(value[None], (devices,) + value.shape)
    return lax.all_to_all(copies, AXES, 0, 0, tiled=True)


def all_sum(value):
    count = lax.axis_size("stream") * lax.axis_size("replica")
    rows, cols = value.shape
    pieces = value.reshape(rows, count, cols // count).transpose(1, 0, 2)
    got = lax.all_to_all(pieces, AXES, 0, 0, tiled=True)
    mine = jnp.sum(got, 0)
    back = spread(mine, count)
    return back.transpose(1, 0, 2).reshape(rows, cols)


def thirds(value):
    high = lax.reduce_precision(value, 8, 7)
    rest = value - high
    mid = lax.reduce_precision(rest, 8, 7)
    low = rest - mid
    return [part.astype(jnp.bfloat16) for part in (high, mid, low)]


def basis_kernel(bounds, left_ref, out_ref):
    blocks = [left_ref[:, lo:hi] for lo, hi in bounds]
    places = lax.broadcasted_iota(jnp.int32, (8, 1), 0)
    for turn in range(8):
        for n, block in enumerate(blocks):
            row = block[turn : turn + 1]
            row = row * lax.rsqrt(jnp.sum(row * row, -1, keepdims=True) + 1e-12)
            shares = jnp.sum(block * row, -1, keepdims=True)
            shares = jnp.where(places > turn, shares, 0.0)
            block = block - shares * row
            blocks[n] = jnp.where(places == turn, row, block)
    for (lo, hi), block in zip(bounds, blocks):
        out_ref[:, lo:hi] = block


def split_rows(value):
    high = value.astype(jnp.bfloat16)
    rest = value - high.astype(jnp.float32)
    mid = rest.astype(jnp.bfloat16)
    low = (rest - mid.astype(jnp.float32)).astype(jnp.bfloat16)
    return [high, mid, low]


def matmul(left, right, contract):
    return lax.dot_general(left, right, (contract, ((), ())), preferred_element_type=jnp.float32)


NN, NT, TN = ((1,), (0,)), ((1,), (1,)), ((0,), (0,))


SPOTS = (0, 3 * D, 4 * D, 4 * D + FF, 5 * D + FF, 6 * D + FF, 7 * D + FF, 8 * D + FF, 9 * D + FF)
SCALE = HDIM ** (-0.5)
TILE = 512


def turn_table():
    freqs = (10000.0 ** (-(np.arange(HDIM // 2).astype(np.float32) * 2.0) / HDIM)).astype(np.float32)
    angle = np.arange(256, dtype=np.float32)[:, None] * freqs[None, :]
    wide = np.concatenate([np.tile(np.cos(angle), 8), np.tile(np.sin(angle), 8)], 1)
    rest = wide.astype(np.float32)
    parts = []
    for _ in range(3):
        part = rest.astype(jnp.bfloat16)
        parts.append(part)
        rest = rest - part.astype(np.float32)
    return np.concatenate(parts, 1)


def lanes(shape):
    return lax.broadcasted_iota(jnp.int32, shape, 1)


def turned(value, cosine, sine, sign):
    first = (lanes(value.shape) % HDIM) < HDIM // 2
    if sign > 0:
        rot = jnp.where(first, -pltpu.roll(value, 112, 1), pltpu.roll(value, 16, 1))
        return value * cosine + rot * sine
    part = value * sine
    return value * cosine + jnp.where(first, pltpu.roll(part, 112, 1), -pltpu.roll(part, 16, 1))


def head_mask(head, rows):
    return (lanes((rows, 128)) // HDIM) == head


def bias(vec_ref, n, width):
    return vec_ref[:, SPOTS[n] : SPOTS[n] + width]


def norm(resid):
    center = resid - jnp.mean(resid, -1, keepdims=True)
    inv_std = lax.rsqrt(jnp.mean(center * center, -1, keepdims=True) + 1e-05)
    return center * inv_std, inv_std


def encode_kernel(first, *refs):
    x_ref, segc_ref, segr_ref, table_ref = refs[:4]
    weights, vec_ref = refs[4:9], refs[9]
    (
        q_ref, k_ref, v_ref, ctx_ref, n1_ref, h1_ref, pre_ref, act_ref, n2_ref, h2_ref, out_ref,
        low_ref, stat_ref, cos_ref, sin_ref,
    ) = refs[10:25]
    if first:
        for w_ref, low in zip(weights, refs[25:30]):
            low[...] = w_ref[...].astype(jnp.bfloat16)
        weights = refs[25:30]
    wqkv_ref, wout_ref, wup_ref, wdown_ref, whead_ref = weights
    count = x_ref.shape[0]
    tile = min(count, TILE)
    starts = [
        jnp.sum((segr_ref[...] < d).astype(jnp.int32), -1, keepdims=True) for d in range(NSEG)
    ]

    def project(t, _):
        rows = pl.ds(pl.multiple_of(t * tile, tile), tile)
        place = t * tile + lax.broadcasted_iota(jnp.int32, (tile, 1), 0)
        for d in range(NSEG):
            place = jnp.where(segc_ref[rows, :] == d, place - starts[d], place)
        hot = (place == lanes((tile, 256))).astype(jnp.float32).astype(jnp.bfloat16)
        both = matmul(hot, table_ref[...], NN)
        both = both[:, :256] + both[:, 256:512] + both[:, 512:]
        cosine, sine = both[:, :128], both[:, 128:]
        cos_ref[rows, :] = cosine
        sin_ref[rows, :] = sine
        x = x_ref[rows, :]
        for part, dst in enumerate((q_ref, k_ref, v_ref)):
            val = matmul(x, wqkv_ref[:, part * D : part * D + D], NN) + vec_ref[:, part * D : part * D + D]
            for g in range(3):
                cols = slice(g * 128, g * 128 + 128)
                piece = val[:, cols]
                if part < 2:
                    piece = turned(piece, cosine, sine, 1)
                dst[rows, cols] = piece.astype(jnp.bfloat16)
        return 0

    lax.fori_loop(0, count // tile, project, 0)

    def rest(t, _):
        rows = pl.ds(pl.multiple_of(t * tile, tile), tile)
        same = segc_ref[rows, :] == segr_ref[...]
        stats = jnp.zeros((tile, 128), jnp.float32)
        for g in range(3):
            cols = slice(g * 128, g * 128 + 128)
            q, k, v = q_ref[rows, cols], k_ref[:, cols], v_ref[:, cols]
            total = jnp.zeros((tile, 128), jnp.float32)
            for h in range(4):
                mine = jnp.where(head_mask(h, tile), q, jnp.zeros_like(q))
                scores = matmul(mine, k, NT) * SCALE
                scores = jnp.where(same, scores, -1e30)
                peak = jnp.max(scores, -1, keepdims=True)
                expo = jnp.exp(scores - peak)
                norm_sum = jnp.sum(expo, -1, keepdims=True)
                probs = (expo * (1.0 / norm_sum)).astype(jnp.bfloat16)
                part = matmul(probs, v, NN)
                total = jnp.where(head_mask(h, tile), part, total)
                stats = jnp.where(lanes((tile, 128)) == g * 4 + h, peak + jnp.log(norm_sum), stats)
            ctx_ref[rows, cols] = total.astype(jnp.bfloat16)
        resid = x_ref[rows, :].astype(jnp.float32) + (
            matmul(ctx_ref[rows, :], wout_ref[...], NN) + bias(vec_ref, 1, D)
        )
        normed, inv_one = norm(resid)
        n1_ref[rows, :] = normed
        hidden = normed * bias(vec_ref, 4, D) + bias(vec_ref, 5, D)
        low = hidden.astype(jnp.bfloat16)
        h1_ref[rows, :] = low
        mixed = jnp.zeros((tile, D), jnp.float32)
        for c in range(4):
            cols = slice(c * D, c * D + D)
            pre = matmul(low, wup_ref[:, cols], NN) + vec_ref[:, SPOTS[2] + c * D : SPOTS[2] + c * D + D]
            pre_ref[rows, cols] = pre
            act = gelu(pre).astype(jnp.bfloat16)
            act_ref[rows, cols] = act
            mixed = mixed + matmul(act, wdown_ref[cols, :], NN)
        normed, inv_two = norm(hidden + (mixed + bias(vec_ref, 3, D)))
        n2_ref[rows, :] = normed
        low = (normed * bias(vec_ref, 6, D) + bias(vec_ref, 7, D)).astype(jnp.bfloat16)
        h2_ref[rows, :] = low
        emitted = matmul(low, whead_ref[...], NT) + vec_ref[:, SPOTS[8] : SPOTS[8] + 96]
        inv_len = lax.rsqrt(jnp.sum(emitted * emitted, -1, keepdims=True) + 1e-06)
        out = emitted * inv_len
        out_ref[rows, :] = out
        low_ref[rows, :] = out.astype(jnp.bfloat16)
        place = lanes((tile, 128))
        stats = jnp.where(place == 12, inv_one, stats)
        stats = jnp.where(place == 13, inv_two, stats)
        stat_ref[rows, :] = jnp.where(place == 14, inv_len, stats)
        return 0

    lax.fori_loop(0, count // tile, rest, 0)


def encode_call(tokens, segment, table, weights, vectors, first, name):
    count = tokens.shape[0]
    f32, low = jnp.float32, jnp.bfloat16
    shapes = [
        (D, low), (D, low), (D, low), (D, low), (D, f32), (D, low), (FF, f32), (FF, low), (D, f32),
        (D, low), (96, f32), (96, low), (128, f32), (128, f32), (128, f32),
    ]
    outs = [jax.ShapeDtypeStruct((count, width), kind) for width, kind in shapes]
    if first:
        outs += [jax.ShapeDtypeStruct(w.shape, low) for w in weights]
    return pl.pallas_call(
        lambda *refs: encode_kernel(first, *refs), out_shape=outs, name=name
    )(tokens, segment[:, None], segment[None, :], table, *weights, vectors)


def backward_kernel(*refs):
    (
        grad_ref, segc_ref, segr_ref, q_ref, k_ref, v_ref, n1_ref, pre_ref, n2_ref, out_ref,
        stat_ref, cos_ref, sin_ref, wqkv_ref, wout_ref, wup_ref, wdown_ref, whead_ref, vec_ref,
    ) = refs[:19]
    yqkv_ref, yout_ref, yup_ref, ydown_ref, yhead_ref, packed_ref = refs[19:25]
    dk_ref, dv_ref, p_ref, s_ref, c_ref = refs[25:]
    count = q_ref.shape[0]
    tile = min(count, TILE)
    packed_ref[...] = jnp.zeros_like(packed_ref)
    dk_ref[...] = jnp.zeros_like(dk_ref)
    dv_ref[...] = jnp.zeros_like(dv_ref)

    def add(n, value, shift=0):
        at = SPOTS[n] + shift
        cols = slice(at, at + value.shape[1])
        packed_ref[:, cols] = packed_ref[:, cols] + jnp.sum(value, 0, keepdims=True)

    def norm_grad(grad, gain, normed, inv_std):
        scaled = grad * gain
        return inv_std * (
            scaled
            - jnp.mean(scaled, -1, keepdims=True)
            - normed * jnp.mean(scaled * normed, -1, keepdims=True)
        )

    def step(t, _):
        rows = pl.ds(pl.multiple_of(t * tile, tile), tile)
        stats = stat_ref[rows, :]
        grad_vec = grad_ref[rows, :] if len(grad_ref.shape) == 2 else jnp.sum(grad_ref[...], 0)
        output = out_ref[rows, :]
        emit = stats[:, 14:15] * (grad_vec - output * jnp.sum(grad_vec * output, -1, keepdims=True))
        add(8, emit)
        low = emit.astype(jnp.bfloat16)
        yhead_ref[rows, :] = low
        grad = matmul(low, whead_ref[...], NN)
        normed = n2_ref[rows, :]
        resid_two = norm_grad(grad, bias(vec_ref, 6, D), normed, stats[:, 13:14])
        add(6, grad * normed)
        add(7, grad)
        add(3, resid_two)
        low = resid_two.astype(jnp.bfloat16)
        ydown_ref[rows, :] = low
        grad = resid_two
        for c in range(4):
            cols = slice(c * D, c * D + D)
            pre = matmul(low, wdown_ref[cols, :], NT) * gelu_slope(pre_ref[rows, cols])
            add(2, pre, c * D)
            pre = pre.astype(jnp.bfloat16)
            yup_ref[rows, cols] = pre
            grad = grad + matmul(pre, wup_ref[:, cols], NT)
        normed = n1_ref[rows, :]
        resid_one = norm_grad(grad, bias(vec_ref, 4, D), normed, stats[:, 12:13])
        add(4, grad * normed)
        add(5, grad)
        add(1, resid_one)
        low = resid_one.astype(jnp.bfloat16)
        yout_ref[rows, :] = low
        grad_ctx = matmul(low, wout_ref[...], NT).astype(jnp.bfloat16)
        same = segc_ref[rows, :] == segr_ref[...]
        cosine, sine = cos_ref[rows, :], sin_ref[rows, :]
        for g in range(3):
            cols = slice(g * 128, g * 128 + 128)
            q, k, v = q_ref[rows, cols], k_ref[:, cols], v_ref[:, cols]
            dctx = grad_ctx[:, cols]
            dq = jnp.zeros((tile, 128), jnp.float32)
            for h in range(4):
                mask = head_mask(h, tile)
                mine = jnp.where(mask, q, jnp.zeros_like(q))
                back = jnp.where(mask, dctx, jnp.zeros_like(dctx))
                place = slice(h * tile, h * tile + tile)
                scores = matmul(mine, k, NT) * SCALE
                head = g * 4 + h
                probs = jnp.where(same, jnp.exp(scores - stats[:, head : head + 1]), 0.0)
                gprob = matmul(back, v, NT)
                weighed = gprob * probs
                gscore = weighed - probs * jnp.sum(weighed, -1, keepdims=True)
                gscore = gscore.astype(jnp.bfloat16)
                p_ref[place, :] = probs.astype(jnp.bfloat16)
                s_ref[place, :] = gscore
                c_ref[place, :] = back
                c_ref[4 * tile + h * tile : 4 * tile + h * tile + tile, :] = mine
                dq = jnp.where(mask, matmul(gscore, k, NN), dq)
            dv_ref[:, cols] = dv_ref[:, cols] + matmul(p_ref[...], c_ref[: 4 * tile, :], TN)
            dk_ref[:, cols] = dk_ref[:, cols] + matmul(s_ref[...], c_ref[4 * tile :, :], TN)
            dq = turned(dq * SCALE, cosine, sine, -1)
            add(0, dq, g * 128)
            yqkv_ref[rows, cols] = dq.astype(jnp.bfloat16)
        return 0

    lax.fori_loop(0, count // tile, step, 0)

    def last(t, _):
        rows = pl.ds(pl.multiple_of(t * tile, tile), tile)
        cosine, sine = cos_ref[rows, :], sin_ref[rows, :]
        for g in range(3):
            cols = slice(g * 128, g * 128 + 128)
            dk = turned(dk_ref[rows, cols] * SCALE, cosine, sine, -1)
            dv = dv_ref[rows, cols]
            add(0, dk, D + g * 128)
            add(0, dv, 2 * D + g * 128)
            yqkv_ref[rows, D + g * 128 : D + g * 128 + 128] = dk.astype(jnp.bfloat16)
            yqkv_ref[rows, 2 * D + g * 128 : 2 * D + g * 128 + 128] = dv.astype(jnp.bfloat16)
        return 0

    lax.fori_loop(0, count // tile, last, 0)


def backward_call(grad, segment, kept, weights, vectors, name):
    q, k, v, _, n1, _, pre, _, n2, _, out, _, stat, cosine, sine = kept
    count = q.shape[0]
    tile = min(count, TILE)
    f32, low = jnp.float32, jnp.bfloat16
    outs = [jax.ShapeDtypeStruct((count, width), low) for width in (3 * D, D, FF, D, 96)]
    return pl.pallas_call(
        backward_kernel,
        out_shape=outs + [jax.ShapeDtypeStruct((1, 5120), f32)],
        scratch_shapes=[
            pltpu.VMEM((count, D), f32),
            pltpu.VMEM((count, D), f32),
            pltpu.VMEM((4 * tile, count), low),
            pltpu.VMEM((4 * tile, count), low),
            pltpu.VMEM((8 * tile, 128), low),
        ],
        name=name,
    )(
        grad, segment[:, None], segment[None, :], q, k, v, n1, pre, n2, out, stat, cosine, sine,
        *weights, vectors,
    )


def early_kernel(me_ref, *refs):
    fac_refs, err_refs, early_ref, parts_ref = refs[:5], refs[5:10], refs[10], refs[11]
    at = to = 0
    for n, (fac_ref, err_ref) in enumerate(zip(fac_refs, err_refs)):
        wide = fac_ref.shape[1]
        head = n == 4
        quarter = (err_ref.shape[1] if head else 4 * err_ref.shape[0]) // 4
        parts = jnp.concatenate(split_rows(fac_ref[...]), 0)
        parts_ref[:, to : to + wide] = parts
        to += wide
        total = jnp.zeros((24, quarter), jnp.float32)
        if head:
            total = jnp.zeros((24, 4 * quarter), jnp.float32)
        for part in split_rows(err_ref[...]):
            total = total + matmul(parts, part, NN if head else NT)
        total = total[:8] + total[8:16] + total[16:24]
        spread_out = total if head else jnp.concatenate([total] * 4, 1)
        spot = lanes(spread_out.shape) // quarter
        early_ref[:, at : at + 4 * quarter] = jnp.where(spot == me_ref[0], spread_out, 0.0)
        at += 4 * quarter


def grads_kernel(me_ref, *refs):
    acts, parts_ref, early_ref, packed_refs = refs[:20], refs[20], refs[21], refs[22:24]
    a_ref, b_ref, left_ref = refs[24:]
    me = me_ref[0]

    def turns(quarter):
        turn = quarter ^ me
        return (turn & 1) * 2 + (turn >> 1), turn

    def place(block, value):
        low = value.astype(jnp.bfloat16)
        for quarter in range(4):
            a_at, b_at = turns(quarter)
            rows = low[quarter * 96 : quarter * 96 + 96]
            if block < 6:
                a_ref[a_at, block * 96 : block * 96 + 96, :] = rows
            elif block < 12:
                b_ref[b_at, (block - 6) * 96 : (block - 6) * 96 + 96, :] = rows
            else:
                b_ref[b_at, 576:600, :] = low[quarter * 24 : quarter * 24 + 24]
                b_ref[b_at, 600:608, :] = jnp.zeros((8, 384), jnp.bfloat16)

    block = at = to = 0
    for n in range(5):
        dx_ref, qx_ref, dy_ref, qy_ref = acts[4 * n : 4 * n + 4]
        parts = parts_ref[:, to : to + dy_ref.shape[1]]
        to += dy_ref.shape[1]
        tall_d = matmul(dy_ref[...], parts, NT)
        tall_q = matmul(qy_ref[...], parts, NT)
        parts = []
        for tall in (tall_d, tall_q):
            tall = tall[:, :8] + tall[:, 8:16] + tall[:, 16:24]
            parts.append(jnp.concatenate(split_rows(tall), 1))
        wide = dx_ref.shape[1]
        left = matmul(parts[0], dx_ref[...], TN) + matmul(parts[1], qx_ref[...], TN)
        left_ref[:, at : at + wide] = (
            left[:8] + left[8:16] + left[16:24] + early_ref[:, at : at + wide]
        )
        at += wide
        if n == 4:
            place(
                block,
                matmul(dy_ref[...], dx_ref[...], TN) + matmul(qy_ref[...], qx_ref[...], TN),
            )
            continue
        for k in range(wide // 384):
            rows = slice(k * 384, k * 384 + 384)
            dxt, qxt = dx_ref[:, rows].T, qx_ref[:, rows].T
            for c in range(dy_ref.shape[1] // 384):
                cols = slice(c * 384, c * 384 + 384)
                place(block, matmul(dxt, dy_ref[:, cols], NN) + matmul(qxt, qy_ref[:, cols], NN))
                block += 1
    side = packed_refs[0].shape[1] // 8
    for r in range(8):
        cols = slice(r * side, r * side + side)
        left_ref[r : r + 1, at : at + side] = packed_refs[0][:, cols] + packed_refs[1][:, cols]
    left_ref[:, at + side :] = jnp.zeros((8, left_ref.shape[1] - at - side), jnp.float32)


def factors_kernel(bounds, me_ref, left_ref, *refs):
    acts, err_refs = refs[:20], refs[20:25]
    basis_ref, right_ref = refs[25:]
    me = me_ref[0]
    basis_kernel(bounds, left_ref, basis_ref)
    at = 0
    for n, (lo, hi) in enumerate(bounds):
        dx_ref, qx_ref, dy_ref, qy_ref = acts[4 * n : 4 * n + 4]
        base = basis_ref[:, lo:hi]
        base_parts = jnp.concatenate(split_rows(base), 0)
        total = None
        for x_ref, y_ref in ((dx_ref, dy_ref), (qx_ref, qy_ref)):
            tall = matmul(x_ref[...], base_parts, NT)
            tall = tall[:, :8] + tall[:, 8:16] + tall[:, 16:24]
            right = matmul(jnp.concatenate(split_rows(tall), 1), y_ref[...], TN)
            total = right if total is None else total + right
        quarter = (hi - lo) // 4
        if n == 4:
            share = jnp.where(lanes(base.shape) // quarter == me, base, 0.0)
        else:
            share = jnp.zeros((8, quarter), jnp.float32)
            for k in range(4):
                share = jnp.where(me == k, base[:, k * quarter : (k + 1) * quarter], share)
        share = jnp.concatenate(split_rows(share), 0)
        for part in split_rows(err_refs[n][...]):
            total = total + matmul(share, part, NT if n == 4 else NN)
        wide = dy_ref.shape[1]
        right_ref[:, at : at + wide] = total[:8] + total[8:16] + total[16:24]
        at += wide
    right_ref[:, at:] = jnp.zeros((8, right_ref.shape[1] - at), jnp.float32)


HEIGHTS = (D, D, D, FF, D)


def weight_kernel(spans, rate, *refs):
    right_ref, summed_ref, vec_ref, vec_mom_ref = refs[:4]
    ins, outs = refs[4:19], refs[19:]
    for n, (at, span) in enumerate(spans):
        basis_ref, mom_ref, w_ref = ins[3 * n : 3 * n + 3]
        new_w_ref, new_m_ref = outs[2 * n : 2 * n + 2]

        def update(approx):
            moved = MOMENTUM * mom_ref[...] + approx
            new_m_ref[...] = moved
            new_w_ref[...] = w_ref[...] - rate * moved

        right = right_ref[:, at : at + span]
        if n < 4:
            update(matmul(basis_ref[...], right, NN))
        else:
            pl.when(pl.program_id(0) == 0)(
                lambda: update(lax.dot_general(
                    right, basis_ref[...], (((0,), (1,)), ((), ())),
                    preferred_element_type=jnp.float32,
                ))
            )

    @pl.when(pl.program_id(0) == 0)
    def _():
        first = sum(HEIGHTS)
        side = 640
        for r in range(8):
            width = min(side, vec_ref.shape[1] - r * side)
            cols = slice(r * side, r * side + width)
            moved = (
                MOMENTUM * vec_mom_ref[:, cols] + summed_ref[r : r + 1, first : first + width]
            )
            outs[11][:, cols] = moved
            outs[10][:, cols] = vec_ref[:, cols] - rate * moved


def error_kernel(spans, replicas, me_ref, right_ref, *refs):
    a_refs, b_refs = refs[:2], refs[2:4]
    basis_refs, err_refs, new_refs = refs[4:9], refs[9:14], refs[14:]
    share = 1.0 / replicas
    quarter = pl.program_id(0)
    turn = quarter ^ me_ref[0]

    def pick(pair, near, rows):
        return jnp.where(near, pair[0][0, rows, :], pair[1][0, rows, :]).astype(jnp.float32)

    def grad(block):
        if block < 6:
            return pick(a_refs, (turn & 1) == 0, slice(block * 96, block * 96 + 96))
        return pick(b_refs, (turn >> 1) == 0, slice((block - 6) * 96, (block - 6) * 96 + 96))

    block = 0
    for n, (at, span) in enumerate(spans):
        right = right_ref[:, at : at + span]
        if n == 3:
            for k in range(4):
                approx = matmul(basis_refs[n][k], right, NN)
                new_refs[n][k] = grad(block) + err_refs[n][k] - approx * share
                block += 1
        elif n == 4:
            approx = lax.dot_general(
                right, basis_refs[n][...], (((0,), (1,)), ((), ())),
                preferred_element_type=jnp.float32,
            )
            base = err_refs[n][...] - approx * share
            near = (turn >> 1) == 0
            rows = pl.ds(pl.multiple_of(quarter * 24, 8), 24)
            new_refs[n][...] = jnp.where(quarter == 0, base, new_refs[n][...])
            new_refs[n][rows, :] = new_refs[n][rows, :] + pick(b_refs, near, slice(576, 600))
        else:
            approx = matmul(basis_refs[n][...], right, NN)
            for c in range(span // 384):
                cols = slice(c * 384, c * 384 + 384)
                new_refs[n][:, cols] = grad(block) + err_refs[n][:, cols] - approx[:, cols] * share
                block += 1


def whole(value):
    return pl.BlockSpec(value.shape, lambda i, me: (0,) * value.ndim)


def exchange(value, turn):
    return lax.ppermute(value, "stream", [(i, i ^ turn) for i in range(4)])


def stream_sum(a, b):
    def add(first, second):
        return (first.astype(jnp.float32) + second.astype(jnp.float32)).astype(jnp.bfloat16)

    both = []
    got = [exchange(a[2:], 1), exchange(b[2:], 2)]
    half = [add(a[:2], got[0]), add(b[:2], got[1])]
    got = [exchange(half[0][1], 2), exchange(half[1][1], 1)]
    full = [add(half[0][0], got[0]), add(half[1][0], got[1])]
    got = [exchange(full[0], 2), exchange(full[1], 1)]
    pair = [jnp.stack([one, two], 0) for one, two in zip(full, got)]
    last = [exchange(pair[0], 1), exchange(pair[1], 2)]
    return pair[0], last[0], pair[1], last[1]


def shards(
    query_embeds,
    doc_embeds,
    doc_segments,
    candidates,
    neg_counts,
    w_qkv,
    w_out,
    w_up,
    w_down,
    w_head,
    vectors,
    mom_qkv,
    mom_out,
    mom_up,
    mom_down,
    mom_head,
    mom_vectors,
    err_qkv,
    err_out,
    err_up,
    err_down,
    err_head,
    fac_qkv,
    fac_out,
    fac_up,
    fac_down,
    fac_head,
):
    streams, replicas = lax.axis_size("stream"), lax.axis_size("replica")
    devices = streams * replicas
    my_stream, me = lax.axis_index("stream"), lax.axis_index(AXES)
    qdev, qlen, width = query_embeds.shape
    row = doc_embeds.shape[1]
    qtok = qdev * qlen
    weights = (w_qkv, w_out, w_up, w_down, w_head.T)
    moms = (mom_qkv, mom_out, mom_up, mom_down, mom_head.T)
    errs = (err_qkv[0], err_out[0], err_up[0], err_down[0], err_head[0].T)
    fac_rows = [fac.T for fac in (fac_qkv, fac_out, fac_up, fac_down, fac_head)]
    sizes = [v.shape for v in (w_qkv, w_out, w_up, w_down, w_head)]
    vec_row = vectors[None, :]
    table = jnp.asarray(turn_table())
    query_in = query_embeds.reshape(qtok, width)
    query_seg = jnp.arange(qtok, dtype=jnp.int32) // qlen
    *query_kept, m0, m1, m2, m3, m4 = encode_call(
        query_in, query_seg, table, weights, vec_row,
        True, "encode_queries",
    )
    mats = (m0, m1, m2, m3, m4)
    all_query = spread(query_kept[11], devices)

    doc_in = doc_embeds[0]
    doc_seg = doc_segments[0]
    doc_kept = encode_call(
        doc_in, doc_seg, table, mats, vec_row, False, "encode_documents"
    )
    doc_low = doc_kept[11]
    pdim = doc_low.shape[1]

    tokens = devices * qtok
    rows_all = all_query.reshape(tokens, pdim)
    segment = doc_segments[0]
    sims = (
        lax.dot_general(
            doc_low, rows_all, (((1,), (1,)), ((), ())), preferred_element_type=jnp.float32
        )
        / SOFT
    )
    weight = jnp.exp(sims)
    segmask = (segment[None, :] == jnp.arange(NSEG)[:, None]).astype(jnp.float32)
    totals = jnp.stack(
        [jnp.sum(jnp.where((segment == d)[:, None], weight, 0.0), 0) for d in range(NSEG)], 0
    )
    scores = (SOFT * jnp.log(totals)).reshape(NSEG, devices, qdev, qlen).sum(-1)
    scores = scores.reshape(NSEG, devices * qdev)
    table = spread(scores, devices).reshape(devices * NSEG, devices * qdev)
    me_stream = my_stream[None].astype(jnp.int32)
    height, wide = sum(m for m, _ in sizes), sum(n for _, n in sizes)
    early, fac_parts = pl.pallas_call(
        early_kernel,
        grid_spec=pltpu.PrefetchScalarGridSpec(
            num_scalar_prefetch=1,
            grid=(1,),
            in_specs=[whole(v) for v in fac_rows]
            + [
                pl.BlockSpec((e.shape[0] // 4, e.shape[1]), lambda i, me: (me[0], 0))
                for e in errs[:4]
            ]
            + [whole(errs[4])],
            out_specs=[
                pl.BlockSpec((8, height), lambda i, me: (0, 0)),
                pl.BlockSpec((24, wide), lambda i, me: (0, 0)),
            ],
        ),
        out_shape=[
            jax.ShapeDtypeStruct((8, height), jnp.float32),
            jax.ShapeDtypeStruct((24, wide), jnp.bfloat16),
        ],
        name="early",
    )(me_stream, *fac_rows, *lax.optimization_barrier((errs, scores))[0])
    docs = jnp.arange(devices * NSEG)
    slots = jnp.arange(candidates.shape[1])
    named = (candidates[None] == docs[:, None, None]) & (slots <= neg_counts[:, None])[None]
    first = (candidates[:, 0][None] == docs[:, None]).astype(jnp.float32)
    listed = jnp.any(named, -1)
    logits = jnp.where(listed, table, -1e30)
    peak = jnp.max(logits, 0, keepdims=True)
    expo = jnp.exp(logits - peak)
    total = jnp.sum(expo, 0, keepdims=True)
    total_queries = candidates.shape[0]
    losses = peak[0] + jnp.log(total[0]) - jnp.sum(table * first, 0)
    loss = jnp.mean(losses)
    grad_table = (expo / total - first) / total_queries
    own = lax.dynamic_slice_in_dim(grad_table, me * NSEG, NSEG, 0)
    per_token = jnp.repeat(own, qlen, axis=1) / totals
    spots = jnp.sum(segmask[:, :, None] * per_token[:, None, :], 0)
    sim_low = (weight * spots).astype(jnp.bfloat16)
    query_grad = lax.dot_general(
        sim_low, doc_low, (((0,), (0,)), ((), ())), preferred_element_type=jnp.float32
    ).reshape(devices, qtok, pdim)
    query_local = lax.all_to_all(query_grad, AXES, 0, 0, tiled=True)
    doc_grad = jnp.dot(sim_low, rows_all, preferred_element_type=jnp.float32)

    *doc_out, doc_packed = backward_call(
        doc_grad, doc_seg, doc_kept, mats, vec_row, "backward_documents"
    )
    *query_out, query_packed = backward_call(
        query_local, query_seg, query_kept, mats, vec_row, "backward_queries"
    )
    inputs = ((doc_in, query_in),) + tuple((doc_kept[n], query_kept[n]) for n in (3, 5, 7, 9))
    acts = [
        v for (dx, qx), dy, qy in zip(inputs, doc_out, query_out) for v in (dx, qx, dy, qy)
    ]
    edges = [0]
    for m, _ in sizes:
        edges.append(edges[-1] + m)
    bounds = list(zip(edges[:-1], edges[1:]))
    side = doc_packed.shape[1] // 8
    full = edges[-1] + side
    full += -full % (128 * devices) if devices <= 32 else -full % (16 * devices)
    a_grads, b_grads, left = pl.pallas_call(
        grads_kernel,
        grid_spec=pltpu.PrefetchScalarGridSpec(
            num_scalar_prefetch=1,
            grid=(1,),
            in_specs=[whole(v) for v in acts + [fac_parts, early, doc_packed, query_packed]],
            out_specs=[
                pl.BlockSpec((4, 576, D), lambda i, me: (0, 0, 0)),
                pl.BlockSpec((4, 608, D), lambda i, me: (0, 0, 0)),
                pl.BlockSpec((8, full), lambda i, me: (0, 0)),
            ],
        ),
        out_shape=[
            jax.ShapeDtypeStruct((4, 576, D), jnp.bfloat16),
            jax.ShapeDtypeStruct((4, 608, D), jnp.bfloat16),
            jax.ShapeDtypeStruct((8, full), jnp.float32),
        ],
        name="grads",
    )(me_stream, *acts, fac_parts, early, doc_packed, query_packed)
    sums = stream_sum(a_grads, b_grads)

    summed = all_sum(left)

    wide += -wide % (128 * devices) if devices <= 32 else -wide % (128 * devices // 8)
    basis, right = pl.pallas_call(
        lambda *refs: factors_kernel(bounds, *refs),
        grid_spec=pltpu.PrefetchScalarGridSpec(
            num_scalar_prefetch=1,
            grid=(1,),
            in_specs=[whole(summed)]
            + [whole(v) for v in acts]
            + [
                pl.BlockSpec((e.shape[0] // 4, e.shape[1]), lambda i, me: (me[0], 0))
                for e in errs[:4]
            ]
            + [whole(errs[4])],
            out_specs=[
                pl.BlockSpec((8, edges[-1]), lambda i, me: (0, 0)),
                pl.BlockSpec((8, wide), lambda i, me: (0, 0)),
            ],
        ),
        out_shape=[
            jax.ShapeDtypeStruct((8, edges[-1]), jnp.float32),
            jax.ShapeDtypeStruct((8, wide), jnp.float32),
        ],
        name="factors",
    )(me_stream, summed, *acts, *errs)
    joined = all_sum(right)
    rights, spans, at = [], [], 0
    for _, n in sizes:
        rights.append(joined[:, at : at + n])
        spans.append((at, n))
        at += n

    rate = RATE * qdev * math.sqrt(devices / (row + qtok))
    firsts, seconds = thirds(basis), thirds(joined)
    left_parts = jnp.concatenate([firsts[k] for k in (0, 0, 1, 0, 1, 2)], 0).T
    right_parts = jnp.concatenate([seconds[k] for k in (0, 1, 0, 2, 1, 0)], 0)
    left_parts = [left_parts[lo:hi] for lo, hi in bounds]
    steps = 6

    def part_spec(value, head):
        if head:
            return pl.BlockSpec(value.shape, lambda i: (0, 0))
        return pl.BlockSpec((value.shape[0] // steps, value.shape[1]), lambda i: (i, 0))

    trios = list(zip(left_parts, moms, weights))
    moved = pl.pallas_call(
        lambda *refs: weight_kernel(spans, rate, *refs),
        grid=(steps,),
        in_specs=[part_spec(v, True) for v in (right_parts, summed, vec_row, vec_row)]
        + [part_spec(v, n == 4) for n, trio in enumerate(trios) for v in trio],
        out_specs=[part_spec(w, n == 4) for n, w in enumerate(weights) for _ in range(2)]
        + [part_spec(vec_row, True)] * 2,
        out_shape=[jax.ShapeDtypeStruct(w.shape, jnp.float32) for w in weights for _ in range(2)]
        + [jax.ShapeDtypeStruct(vec_row.shape, jnp.float32)] * 2,
        name="weights",
    )(right_parts, summed, vec_row, mom_vectors[None, :], *[v for trio in trios for v in trio])
    new_w, new_m = list(moved[0:10:2]), list(moved[1:10:2])
    new_w[4], new_m[4] = new_w[4].T, new_m[4].T
    new_vec, vec_mom = moved[10][0], moved[11][0]

    def quartered(value):
        if value.shape[0] == 4 * D:
            return value.reshape(4, D, value.shape[1])
        return value

    def quarter_spec(value):
        if len(value.shape) == 3:
            return pl.BlockSpec((4, D // 4, value.shape[2]), lambda q, me: (0, q, 0))
        if value.shape[0] != D or value is left_parts[4]:
            return pl.BlockSpec(value.shape, lambda q, me: (0, 0))
        return pl.BlockSpec((D // 4, value.shape[1]), lambda q, me: (q, 0))

    rows = [quartered(v) for v in left_parts] + [quartered(v) for v in errs]
    out = [jax.ShapeDtypeStruct(quartered(e).shape, jnp.float32) for e in errs]
    new_e = pl.pallas_call(
        lambda *refs: error_kernel(spans, replicas, *refs),
        grid_spec=pltpu.PrefetchScalarGridSpec(
            num_scalar_prefetch=1,
            grid=(4,),
            in_specs=[
                pl.BlockSpec(right_parts.shape, lambda q, me: (0, 0)),
                pl.BlockSpec((1, 576, D), lambda q, me: ((q ^ me[0]) >> 1, 0, 0)),
                pl.BlockSpec((1, 576, D), lambda q, me: ((q ^ me[0]) >> 1, 0, 0)),
                pl.BlockSpec((1, 608, D), lambda q, me: ((q ^ me[0]) & 1, 0, 0)),
                pl.BlockSpec((1, 608, D), lambda q, me: ((q ^ me[0]) & 1, 0, 0)),
            ]
            + [quarter_spec(v) for v in rows],
            out_specs=[quarter_spec(v) for v in out],
        ),
        out_shape=out,
        name="errors",
    )(me_stream, right_parts, *sums, *rows)
    new_e = [v.reshape((1,) + e.shape) for v, e in zip(new_e, errs)]
    new_e[4] = jnp.swapaxes(new_e[4], 1, 2)
    return (
        loss,
        *new_w,
        new_vec,
        *new_m,
        vec_mom,
        *new_e,
        *[right.T for right in rights],
    )


def solution(mesh):
    return jax.shard_map(
        shards,
        mesh=mesh,
        in_specs=(
            P(("stream", "replica"), None, None),
            P(("stream", "replica"), None, None),
            P(("stream", "replica"), None),
            P(),
            P(),
            P(),
            P(),
            P(),
            P(),
            P(),
            P(),
            P(),
            P(),
            P(),
            P(),
            P(),
            P(),
            P("replica", None, None),
            P("replica", None, None),
            P("replica", None, None),
            P("replica", None, None),
            P("replica", None, None),
            P(),
            P(),
            P(),
            P(),
            P(),
        ),
        out_specs=(
            P(),
            P(),
            P(),
            P(),
            P(),
            P(),
            P(),
            P(),
            P(),
            P(),
            P(),
            P(),
            P(),
            P("replica", None, None),
            P("replica", None, None),
            P("replica", None, None),
            P("replica", None, None),
            P("replica", None, None),
            P(),
            P(),
            P(),
            P(),
            P(),
        ),
        check_vma=False,
    )
```

```python
import math

import jax
import jax.numpy as jnp
import numpy as np
from jax import lax
from jax.experimental import pallas as pl
from jax.experimental.pallas import tpu as pltpu
from jax.sharding import PartitionSpec as P

D = 384
HDIM = 32
FF = 1536
NSEG = 4


SOFT = 0.03
MOMENTUM = 0.9
RATE = 0.1


def gelu(value):
    return 0.5 * value * (1.0 + jax.scipy.special.erf(value * 0.7071067811865476))


def gelu_slope(value):
    return (
        0.5 * (1.0 + jax.scipy.special.erf(value * 0.7071067811865476))
        + value * jnp.exp(-0.5 * value * value) * 0.3989422804014327
    )


AXES = ("stream", "replica")


def spread(value, devices):
    copies = jnp.broadcast_to(value[None], (devices,) + value.shape)
    return lax.all_to_all(copies, AXES, 0, 0, tiled=True)


def sum_piece(value):
    count = lax.axis_size("stream") * lax.axis_size("replica")
    rows, cols = value.shape
    pieces = value.reshape(rows, count, cols // count).transpose(1, 0, 2)
    return jnp.sum(lax.all_to_all(pieces, AXES, 0, 0, tiled=True), 0)


def join_pieces(mine):
    count = lax.axis_size("stream") * lax.axis_size("replica")
    return spread(mine, count).transpose(1, 0, 2).reshape(mine.shape[0], -1)


def thirds(value):
    high = lax.reduce_precision(value, 8, 7)
    rest = value - high
    mid = lax.reduce_precision(rest, 8, 7)
    low = rest - mid
    return [part.astype(jnp.bfloat16) for part in (high, mid, low)]


def basis_kernel(bounds, left_ref, out_ref):
    blocks = [left_ref[:, lo:hi] for lo, hi in bounds]
    places = lax.broadcasted_iota(jnp.int32, (8, 1), 0)
    for turn in range(8):
        for n, block in enumerate(blocks):
            row = block[turn : turn + 1]
            row = row * lax.rsqrt(jnp.sum(row * row, -1, keepdims=True) + 1e-12)
            shares = jnp.sum(block * row, -1, keepdims=True)
            shares = jnp.where(places > turn, shares, 0.0)
            block = block - shares * row
            blocks[n] = jnp.where(places == turn, row, block)
    for (lo, hi), block in zip(bounds, blocks):
        out_ref[:, lo:hi] = block


def split_rows(value):
    high = value.astype(jnp.bfloat16)
    rest = value - high.astype(jnp.float32)
    mid = rest.astype(jnp.bfloat16)
    low = (rest - mid.astype(jnp.float32)).astype(jnp.bfloat16)
    return [high, mid, low]


def matmul(left, right, contract):
    return lax.dot_general(left, right, (contract, ((), ())), preferred_element_type=jnp.float32)


NN, NT, TN = ((1,), (0,)), ((1,), (1,)), ((0,), (0,))


SPOTS = (0, 3 * D, 4 * D, 4 * D + FF, 5 * D + FF, 6 * D + FF, 7 * D + FF, 8 * D + FF, 9 * D + FF)
SCALE = HDIM ** (-0.5)
TILE = 512


def turn_table():
    freqs = (10000.0 ** (-(np.arange(HDIM // 2).astype(np.float32) * 2.0) / HDIM)).astype(np.float32)
    angle = np.arange(256, dtype=np.float32)[:, None] * freqs[None, :]
    wide = np.concatenate([np.tile(np.cos(angle), 8), np.tile(np.sin(angle), 8)], 1)
    rest = wide.astype(np.float32)
    parts = []
    for _ in range(3):
        part = rest.astype(jnp.bfloat16)
        parts.append(part)
        rest = rest - part.astype(np.float32)
    return np.concatenate(parts, 1)


def lanes(shape):
    return lax.broadcasted_iota(jnp.int32, shape, 1)


def turned(value, cosine, sine, sign):
    first = (lanes(value.shape) % HDIM) < HDIM // 2
    if sign > 0:
        rot = jnp.where(first, -pltpu.roll(value, 112, 1), pltpu.roll(value, 16, 1))
        return value * cosine + rot * sine
    part = value * sine
    return value * cosine + jnp.where(first, pltpu.roll(part, 112, 1), -pltpu.roll(part, 16, 1))


def head_mask(head, rows):
    return (lanes((rows, 128)) // HDIM) == head


def bias(vec_ref, n, width):
    return vec_ref[:, SPOTS[n] : SPOTS[n] + width]


def norm(resid):
    center = resid - jnp.mean(resid, -1, keepdims=True)
    inv_std = lax.rsqrt(jnp.mean(center * center, -1, keepdims=True) + 1e-05)
    return center * inv_std, inv_std


def encode_kernel(first, *refs):
    x_ref, segc_ref, segr_ref, table_ref = refs[:4]
    weights, vec_ref = refs[4:9], refs[9]
    (
        q_ref, k_ref, v_ref, ctx_ref, n1_ref, h1_ref, pre_ref, act_ref, n2_ref, h2_ref, out_ref,
        low_ref, stat_ref, cos_ref, sin_ref,
    ) = refs[10:25]
    if first:
        for w_ref, low in zip(weights, refs[25:30]):
            low[...] = w_ref[...].astype(jnp.bfloat16)
        weights = refs[25:30]
    wqkv_ref, wout_ref, wup_ref, wdown_ref, whead_ref = weights
    count = x_ref.shape[0]
    tile = min(count, TILE)
    starts = [
        jnp.sum((segr_ref[...] < d).astype(jnp.int32), -1, keepdims=True) for d in range(NSEG)
    ]

    def project(t, _):
        rows = pl.ds(pl.multiple_of(t * tile, tile), tile)
        place = t * tile + lax.broadcasted_iota(jnp.int32, (tile, 1), 0)
        for d in range(NSEG):
            place = jnp.where(segc_ref[rows, :] == d, place - starts[d], place)
        hot = (place == lanes((tile, 256))).astype(jnp.float32).astype(jnp.bfloat16)
        both = matmul(hot, table_ref[...], NN)
        both = both[:, :256] + both[:, 256:512] + both[:, 512:]
        cosine, sine = both[:, :128], both[:, 128:]
        cos_ref[rows, :] = cosine
        sin_ref[rows, :] = sine
        x = x_ref[rows, :]
        for part, dst in enumerate((q_ref, k_ref, v_ref)):
            val = matmul(x, wqkv_ref[:, part * D : part * D + D], NN) + vec_ref[:, part * D : part * D + D]
            for g in range(3):
                cols = slice(g * 128, g * 128 + 128)
                piece = val[:, cols]
                if part < 2:
                    piece = turned(piece, cosine, sine, 1)
                dst[rows, cols] = piece.astype(jnp.bfloat16)
        return 0

    lax.fori_loop(0, count // tile, project, 0)

    def rest(t, _):
        rows = pl.ds(pl.multiple_of(t * tile, tile), tile)
        same = segc_ref[rows, :] == segr_ref[...]
        stats = jnp.zeros((tile, 128), jnp.float32)
        for g in range(3):
            cols = slice(g * 128, g * 128 + 128)
            q, k, v = q_ref[rows, cols], k_ref[:, cols], v_ref[:, cols]
            total = jnp.zeros((tile, 128), jnp.float32)
            for h in range(4):
                mine = jnp.where(head_mask(h, tile), q, jnp.zeros_like(q))
                scores = matmul(mine, k, NT) * SCALE
                scores = jnp.where(same, scores, -1e30)
                peak = jnp.max(scores, -1, keepdims=True)
                expo = jnp.exp(scores - peak)
                norm_sum = jnp.sum(expo, -1, keepdims=True)
                probs = (expo * (1.0 / norm_sum)).astype(jnp.bfloat16)
                part = matmul(probs, v, NN)
                total = jnp.where(head_mask(h, tile), part, total)
                stats = jnp.where(lanes((tile, 128)) == g * 4 + h, peak + jnp.log(norm_sum), stats)
            ctx_ref[rows, cols] = total.astype(jnp.bfloat16)
        resid = x_ref[rows, :].astype(jnp.float32) + (
            matmul(ctx_ref[rows, :], wout_ref[...], NN) + bias(vec_ref, 1, D)
        )
        normed, inv_one = norm(resid)
        n1_ref[rows, :] = normed
        hidden = normed * bias(vec_ref, 4, D) + bias(vec_ref, 5, D)
        low = hidden.astype(jnp.bfloat16)
        h1_ref[rows, :] = low
        mixed = jnp.zeros((tile, D), jnp.float32)
        for c in range(4):
            cols = slice(c * D, c * D + D)
            pre = matmul(low, wup_ref[:, cols], NN) + vec_ref[:, SPOTS[2] + c * D : SPOTS[2] + c * D + D]
            pre_ref[rows, cols] = pre
            act = gelu(pre).astype(jnp.bfloat16)
            act_ref[rows, cols] = act
            mixed = mixed + matmul(act, wdown_ref[cols, :], NN)
        normed, inv_two = norm(hidden + (mixed + bias(vec_ref, 3, D)))
        n2_ref[rows, :] = normed
        low = (normed * bias(vec_ref, 6, D) + bias(vec_ref, 7, D)).astype(jnp.bfloat16)
        h2_ref[rows, :] = low
        emitted = matmul(low, whead_ref[...], NT) + vec_ref[:, SPOTS[8] : SPOTS[8] + 96]
        inv_len = lax.rsqrt(jnp.sum(emitted * emitted, -1, keepdims=True) + 1e-06)
        out = emitted * inv_len
        out_ref[rows, :] = out
        low_ref[rows, :] = out.astype(jnp.bfloat16)
        place = lanes((tile, 128))
        stats = jnp.where(place == 12, inv_one, stats)
        stats = jnp.where(place == 13, inv_two, stats)
        stat_ref[rows, :] = jnp.where(place == 14, inv_len, stats)
        return 0

    lax.fori_loop(0, count // tile, rest, 0)


def encode_call(tokens, segment, table, weights, vectors, first):
    count = tokens.shape[0]
    f32, low = jnp.float32, jnp.bfloat16
    shapes = [
        (D, low), (D, low), (D, low), (D, low), (D, f32), (D, low), (FF, f32), (FF, low), (D, f32),
        (D, low), (96, f32), (96, low), (128, f32), (128, f32), (128, f32),
    ]
    outs = [jax.ShapeDtypeStruct((count, width), kind) for width, kind in shapes]
    if first:
        outs += [jax.ShapeDtypeStruct(w.shape, low) for w in weights]
    return pl.pallas_call(
        lambda *refs: encode_kernel(first, *refs), out_shape=outs
    )(tokens, segment[:, None], segment[None, :], table, *weights, vectors)


def backward_kernel(*refs):
    (
        grad_ref, segc_ref, segr_ref, q_ref, k_ref, v_ref, n1_ref, pre_ref, n2_ref, out_ref,
        stat_ref, cos_ref, sin_ref, _, wout_ref, wup_ref, wdown_ref, whead_ref, vec_ref,
    ) = refs[:19]
    yqkv_ref, yout_ref, yup_ref, ydown_ref, yhead_ref, packed_ref = refs[19:25]
    dk_ref, dv_ref, p_ref, s_ref, c_ref = refs[25:]
    count = q_ref.shape[0]
    tile = min(count, TILE)
    packed_ref[...] = jnp.zeros_like(packed_ref)
    dk_ref[...] = jnp.zeros_like(dk_ref)
    dv_ref[...] = jnp.zeros_like(dv_ref)

    def add(n, value, shift=0):
        at = SPOTS[n] + shift
        cols = slice(at, at + value.shape[1])
        packed_ref[:, cols] = packed_ref[:, cols] + jnp.sum(value, 0, keepdims=True)

    def norm_grad(grad, gain, normed, inv_std):
        scaled = grad * gain
        return inv_std * (
            scaled
            - jnp.mean(scaled, -1, keepdims=True)
            - normed * jnp.mean(scaled * normed, -1, keepdims=True)
        )

    def step(t, _):
        rows = pl.ds(pl.multiple_of(t * tile, tile), tile)
        stats = stat_ref[rows, :]
        grad_vec = grad_ref[rows, :] if len(grad_ref.shape) == 2 else jnp.sum(grad_ref[...], 0)
        output = out_ref[rows, :]
        emit = stats[:, 14:15] * (grad_vec - output * jnp.sum(grad_vec * output, -1, keepdims=True))
        add(8, emit)
        low = emit.astype(jnp.bfloat16)
        yhead_ref[rows, :] = low
        grad = matmul(low, whead_ref[...], NN)
        normed = n2_ref[rows, :]
        resid_two = norm_grad(grad, bias(vec_ref, 6, D), normed, stats[:, 13:14])
        add(6, grad * normed)
        add(7, grad)
        add(3, resid_two)
        low = resid_two.astype(jnp.bfloat16)
        ydown_ref[rows, :] = low
        grad = resid_two
        for c in range(4):
            cols = slice(c * D, c * D + D)
            pre = matmul(low, wdown_ref[cols, :], NT) * gelu_slope(pre_ref[rows, cols])
            add(2, pre, c * D)
            pre = pre.astype(jnp.bfloat16)
            yup_ref[rows, cols] = pre
            grad = grad + matmul(pre, wup_ref[:, cols], NT)
        normed = n1_ref[rows, :]
        resid_one = norm_grad(grad, bias(vec_ref, 4, D), normed, stats[:, 12:13])
        add(4, grad * normed)
        add(5, grad)
        add(1, resid_one)
        low = resid_one.astype(jnp.bfloat16)
        yout_ref[rows, :] = low
        grad_ctx = matmul(low, wout_ref[...], NT).astype(jnp.bfloat16)
        same = segc_ref[rows, :] == segr_ref[...]
        cosine, sine = cos_ref[rows, :], sin_ref[rows, :]
        for g in range(3):
            cols = slice(g * 128, g * 128 + 128)
            q, k, v = q_ref[rows, cols], k_ref[:, cols], v_ref[:, cols]
            dctx = grad_ctx[:, cols]
            dq = jnp.zeros((tile, 128), jnp.float32)
            for h in range(4):
                mask = head_mask(h, tile)
                mine = jnp.where(mask, q, jnp.zeros_like(q))
                back = jnp.where(mask, dctx, jnp.zeros_like(dctx))
                place = slice(h * tile, h * tile + tile)
                scores = matmul(mine, k, NT) * SCALE
                head = g * 4 + h
                probs = jnp.where(same, jnp.exp(scores - stats[:, head : head + 1]), 0.0)
                gprob = matmul(back, v, NT)
                weighed = gprob * probs
                gscore = weighed - probs * jnp.sum(weighed, -1, keepdims=True)
                gscore = gscore.astype(jnp.bfloat16)
                p_ref[place, :] = probs.astype(jnp.bfloat16)
                s_ref[place, :] = gscore
                c_ref[place, :] = back
                c_ref[4 * tile + h * tile : 4 * tile + h * tile + tile, :] = mine
                dq = jnp.where(mask, matmul(gscore, k, NN), dq)
            dv_ref[:, cols] = dv_ref[:, cols] + matmul(p_ref[...], c_ref[: 4 * tile, :], TN)
            dk_ref[:, cols] = dk_ref[:, cols] + matmul(s_ref[...], c_ref[4 * tile :, :], TN)
            dq = turned(dq * SCALE, cosine, sine, -1)
            add(0, dq, g * 128)
            yqkv_ref[rows, cols] = dq.astype(jnp.bfloat16)
        return 0

    lax.fori_loop(0, count // tile, step, 0)

    def last(t, _):
        rows = pl.ds(pl.multiple_of(t * tile, tile), tile)
        cosine, sine = cos_ref[rows, :], sin_ref[rows, :]
        for g in range(3):
            cols = slice(g * 128, g * 128 + 128)
            dk = turned(dk_ref[rows, cols] * SCALE, cosine, sine, -1)
            dv = dv_ref[rows, cols]
            add(0, dk, D + g * 128)
            add(0, dv, 2 * D + g * 128)
            yqkv_ref[rows, D + g * 128 : D + g * 128 + 128] = dk.astype(jnp.bfloat16)
            yqkv_ref[rows, 2 * D + g * 128 : 2 * D + g * 128 + 128] = dv.astype(jnp.bfloat16)
        return 0

    lax.fori_loop(0, count // tile, last, 0)


def backward_call(grad, segment, kept, weights, vectors):
    q, k, v, _, n1, _, pre, _, n2, _, out, _, stat, cosine, sine = kept
    count = q.shape[0]
    tile = min(count, TILE)
    f32, low = jnp.float32, jnp.bfloat16
    outs = [jax.ShapeDtypeStruct((count, width), low) for width in (3 * D, D, FF, D, 96)]
    return pl.pallas_call(
        backward_kernel,
        out_shape=outs + [jax.ShapeDtypeStruct((1, 5120), f32)],
        scratch_shapes=[
            pltpu.VMEM((count, D), f32),
            pltpu.VMEM((count, D), f32),
            pltpu.VMEM((4 * tile, count), low),
            pltpu.VMEM((4 * tile, count), low),
            pltpu.VMEM((8 * tile, 128), low),
        ],
    )(
        grad, segment[:, None], segment[None, :], q, k, v, n1, pre, n2, out, stat, cosine, sine,
        *weights, vectors,
    )


def early_kernel(me_ref, *refs):
    fac_refs, err_refs, early_ref, parts_ref = refs[:5], refs[5:10], refs[10], refs[11]
    at = to = 0
    for n, (fac_ref, err_ref) in enumerate(zip(fac_refs, err_refs)):
        wide = fac_ref.shape[1]
        head = n == 4
        quarter = (err_ref.shape[1] if head else 4 * err_ref.shape[0]) // 4
        parts = jnp.concatenate(split_rows(fac_ref[...]), 0)
        parts_ref[:, to : to + wide] = parts
        to += wide
        total = jnp.zeros((24, quarter), jnp.float32)
        if head:
            total = jnp.zeros((24, 4 * quarter), jnp.float32)
        for part in split_rows(err_ref[...]):
            total = total + matmul(parts, part, NN if head else NT)
        total = total[:8] + total[8:16] + total[16:24]
        spread_out = total if head else jnp.concatenate([total] * 4, 1)
        spot = lanes(spread_out.shape) // quarter
        early_ref[:, at : at + 4 * quarter] = jnp.where(spot == me_ref[0], spread_out, 0.0)
        at += 4 * quarter


def grads_kernel(me_ref, *refs):
    acts, parts_ref, early_ref, packed_refs = refs[:20], refs[20], refs[21], refs[22:24]
    a_ref, b_ref, left_ref = refs[24:]
    me = me_ref[0]

    def turns(quarter):
        turn = quarter ^ me
        return (turn & 1) * 2 + (turn >> 1), turn

    def place(block, value):
        low = value.astype(jnp.bfloat16)
        for quarter in range(4):
            a_at, b_at = turns(quarter)
            rows = low[quarter * 96 : quarter * 96 + 96]
            if block < 6:
                a_ref[a_at, block * 96 : block * 96 + 96, :] = rows
            elif block < 12:
                b_ref[b_at, (block - 6) * 96 : (block - 6) * 96 + 96, :] = rows
            else:
                b_ref[b_at, 576:600, :] = low[quarter * 24 : quarter * 24 + 24]
                b_ref[b_at, 600:608, :] = jnp.zeros((8, 384), jnp.bfloat16)

    block = at = to = 0
    for n in range(5):
        dx_ref, qx_ref, dy_ref, qy_ref = acts[4 * n : 4 * n + 4]
        parts = parts_ref[:, to : to + dy_ref.shape[1]]
        to += dy_ref.shape[1]
        tall_d = matmul(dy_ref[...], parts, NT)
        tall_q = matmul(qy_ref[...], parts, NT)
        parts = []
        for tall in (tall_d, tall_q):
            tall = tall[:, :8] + tall[:, 8:16] + tall[:, 16:24]
            parts.append(jnp.concatenate(split_rows(tall), 1))
        wide = dx_ref.shape[1]
        left = matmul(parts[0], dx_ref[...], TN) + matmul(parts[1], qx_ref[...], TN)
        left_ref[:, at : at + wide] = (
            left[:8] + left[8:16] + left[16:24] + early_ref[:, at : at + wide]
        )
        at += wide
        if n == 4:
            place(
                block,
                matmul(dy_ref[...], dx_ref[...], TN) + matmul(qy_ref[...], qx_ref[...], TN),
            )
            continue
        for k in range(wide // 384):
            rows = slice(k * 384, k * 384 + 384)
            dxt, qxt = dx_ref[:, rows].T, qx_ref[:, rows].T
            for c in range(dy_ref.shape[1] // 384):
                cols = slice(c * 384, c * 384 + 384)
                place(block, matmul(dxt, dy_ref[:, cols], NN) + matmul(qxt, qy_ref[:, cols], NN))
                block += 1
    side = packed_refs[0].shape[1] // 8
    for r in range(8):
        cols = slice(r * side, r * side + side)
        left_ref[r : r + 1, at : at + side] = packed_refs[0][:, cols] + packed_refs[1][:, cols]
    left_ref[:, at + side :] = jnp.zeros((8, left_ref.shape[1] - at - side), jnp.float32)


def factors_kernel(bounds, me_ref, left_ref, *refs):
    acts, err_refs = refs[:20], refs[20:25]
    basis_ref, right_ref = refs[25:]
    me = me_ref[0]
    basis_kernel(bounds, left_ref, basis_ref)
    at = 0
    for n, (lo, hi) in enumerate(bounds):
        dx_ref, qx_ref, dy_ref, qy_ref = acts[4 * n : 4 * n + 4]
        base = basis_ref[:, lo:hi]
        base_parts = jnp.concatenate(split_rows(base), 0)
        total = None
        for x_ref, y_ref in ((dx_ref, dy_ref), (qx_ref, qy_ref)):
            tall = matmul(x_ref[...], base_parts, NT)
            tall = tall[:, :8] + tall[:, 8:16] + tall[:, 16:24]
            right = matmul(jnp.concatenate(split_rows(tall), 1), y_ref[...], TN)
            total = right if total is None else total + right
        quarter = (hi - lo) // 4
        if n == 4:
            share = jnp.where(lanes(base.shape) // quarter == me, base, 0.0)
        else:
            share = jnp.zeros((8, quarter), jnp.float32)
            for k in range(4):
                share = jnp.where(me == k, base[:, k * quarter : (k + 1) * quarter], share)
        share = jnp.concatenate(split_rows(share), 0)
        for part in split_rows(err_refs[n][...]):
            total = total + matmul(share, part, NT if n == 4 else NN)
        wide = dy_ref.shape[1]
        right_ref[:, at : at + wide] = total[:8] + total[8:16] + total[16:24]
        at += wide
    right_ref[:, at:] = jnp.zeros((8, right_ref.shape[1] - at), jnp.float32)


HEIGHTS = (D, D, D, FF, D)


def weight_kernel(spans, rate, *refs):
    right_ref, summed_ref, vec_ref, vec_mom_ref = refs[:4]
    ins, outs = refs[4:19], refs[19:]
    for n, (at, span) in enumerate(spans):
        basis_ref, mom_ref, w_ref = ins[3 * n : 3 * n + 3]
        new_w_ref, new_m_ref = outs[2 * n : 2 * n + 2]

        def update(approx):
            moved = MOMENTUM * mom_ref[...] + approx
            new_m_ref[...] = moved
            new_w_ref[...] = w_ref[...] - rate * moved

        right = right_ref[:, at : at + span]
        if n < 4:
            update(matmul(basis_ref[...], right, NN))
        else:
            pl.when(pl.program_id(0) == 0)(
                lambda: update(lax.dot_general(
                    right, basis_ref[...], (((0,), (1,)), ((), ())),
                    preferred_element_type=jnp.float32,
                ))
            )

    @pl.when(pl.program_id(0) == 0)
    def _():
        first = sum(HEIGHTS)
        side = 640
        for r in range(8):
            width = min(side, vec_ref.shape[1] - r * side)
            cols = slice(r * side, r * side + width)
            moved = (
                MOMENTUM * vec_mom_ref[:, cols] + summed_ref[r : r + 1, first : first + width]
            )
            outs[11][:, cols] = moved
            outs[10][:, cols] = vec_ref[:, cols] - rate * moved


def error_kernel(spans, replicas, me_ref, right_ref, *refs):
    a_refs, b_refs = refs[:2], refs[2:4]
    basis_refs, err_refs, new_refs = refs[4:9], refs[9:14], refs[14:]
    share = 1.0 / replicas
    quarter = pl.program_id(0)
    turn = quarter ^ me_ref[0]

    def pick(pair, near, rows):
        return jnp.where(near, pair[0][0, rows, :], pair[1][0, rows, :]).astype(jnp.float32)

    def grad(block):
        if block < 6:
            return pick(a_refs, (turn & 1) == 0, slice(block * 96, block * 96 + 96))
        return pick(b_refs, (turn >> 1) == 0, slice((block - 6) * 96, (block - 6) * 96 + 96))

    block = 0
    for n, (at, span) in enumerate(spans):
        right = right_ref[:, at : at + span]
        if n == 3:
            for k in range(4):
                approx = matmul(basis_refs[n][k], right, NN)
                new_refs[n][k] = grad(block) + err_refs[n][k] - approx * share
                block += 1
        elif n == 4:
            approx = lax.dot_general(
                right, basis_refs[n][...], (((0,), (1,)), ((), ())),
                preferred_element_type=jnp.float32,
            )
            base = err_refs[n][...] - approx * share
            near = (turn >> 1) == 0
            rows = pl.ds(pl.multiple_of(quarter * 24, 8), 24)
            new_refs[n][...] = jnp.where(quarter == 0, base, new_refs[n][...])
            new_refs[n][rows, :] = new_refs[n][rows, :] + pick(b_refs, near, slice(576, 600))
        else:
            approx = matmul(basis_refs[n][...], right, NN)
            for c in range(span // 384):
                cols = slice(c * 384, c * 384 + 384)
                new_refs[n][:, cols] = grad(block) + err_refs[n][:, cols] - approx[:, cols] * share
                block += 1


def whole(value):
    return pl.BlockSpec(value.shape, lambda i, me: (0,) * value.ndim)


def exchange(value, turn):
    return lax.ppermute(value, "stream", [(i, i ^ turn) for i in range(4)])


def add(first, second):
    return (first.astype(jnp.float32) + second.astype(jnp.float32)).astype(jnp.bfloat16)


def shards(
    query_embeds,
    doc_embeds,
    doc_segments,
    candidates,
    neg_counts,
    w_qkv,
    w_out,
    w_up,
    w_down,
    w_head,
    vectors,
    mom_qkv,
    mom_out,
    mom_up,
    mom_down,
    mom_head,
    mom_vectors,
    err_qkv,
    err_out,
    err_up,
    err_down,
    err_head,
    fac_qkv,
    fac_out,
    fac_up,
    fac_down,
    fac_head,
):
    streams, replicas = lax.axis_size("stream"), lax.axis_size("replica")
    devices = streams * replicas
    my_stream, me = lax.axis_index("stream"), lax.axis_index(AXES)
    qdev, qlen, width = query_embeds.shape
    row = doc_embeds.shape[1]
    qtok = qdev * qlen
    weights = (w_qkv, w_out, w_up, w_down, w_head.T)
    moms = (mom_qkv, mom_out, mom_up, mom_down, mom_head.T)
    errs = (err_qkv[0], err_out[0], err_up[0], err_down[0], err_head[0].T)
    fac_rows = [fac.T for fac in (fac_qkv, fac_out, fac_up, fac_down, fac_head)]
    sizes = [v.shape for v in (w_qkv, w_out, w_up, w_down, w_head)]
    vec_row = vectors[None, :]
    table = jnp.asarray(turn_table())
    query_in = query_embeds.reshape(qtok, width)
    query_seg = jnp.arange(qtok, dtype=jnp.int32) // qlen
    *query_kept, m0, m1, m2, m3, m4 = encode_call(
        query_in, query_seg, table, weights, vec_row,
        True,
    )
    mats = (m0, m1, m2, m3, m4)
    all_query = spread(query_kept[11], devices)

    doc_in = doc_embeds[0]
    doc_seg = doc_segments[0]
    doc_kept = encode_call(doc_in, doc_seg, table, mats, vec_row, False)
    doc_low = doc_kept[11]
    pdim = doc_low.shape[1]

    tokens = devices * qtok
    rows_all = all_query.reshape(tokens, pdim)
    segment = doc_segments[0]
    sims = (
        lax.dot_general(
            doc_low, rows_all, (((1,), (1,)), ((), ())), preferred_element_type=jnp.float32
        )
        / SOFT
    )
    weight = jnp.exp(sims)
    segmask = (segment[None, :] == jnp.arange(NSEG)[:, None]).astype(jnp.float32)
    totals = jnp.stack(
        [jnp.sum(jnp.where((segment == d)[:, None], weight, 0.0), 0) for d in range(NSEG)], 0
    )
    scores = (SOFT * jnp.log(totals)).reshape(NSEG, devices, qdev, qlen).sum(-1)
    scores = scores.reshape(NSEG, devices * qdev)
    table = spread(scores, devices).reshape(devices * NSEG, devices * qdev)
    me_stream = my_stream[None].astype(jnp.int32)
    height, wide = sum(m for m, _ in sizes), sum(n for _, n in sizes)
    early, fac_parts = pl.pallas_call(
        early_kernel,
        grid_spec=pltpu.PrefetchScalarGridSpec(
            num_scalar_prefetch=1,
            grid=(1,),
            in_specs=[whole(v) for v in fac_rows]
            + [
                pl.BlockSpec((e.shape[0] // 4, e.shape[1]), lambda i, me: (me[0], 0))
                for e in errs[:4]
            ]
            + [whole(errs[4])],
            out_specs=[
                pl.BlockSpec((8, height), lambda i, me: (0, 0)),
                pl.BlockSpec((24, wide), lambda i, me: (0, 0)),
            ],
        ),
        out_shape=[
            jax.ShapeDtypeStruct((8, height), jnp.float32),
            jax.ShapeDtypeStruct((24, wide), jnp.bfloat16),
        ],
        name="early",
    )(me_stream, *fac_rows, *lax.optimization_barrier((errs, scores))[0])
    docs = jnp.arange(devices * NSEG)
    slots = jnp.arange(candidates.shape[1])
    named = (candidates[None] == docs[:, None, None]) & (slots <= neg_counts[:, None])[None]
    first = (candidates[:, 0][None] == docs[:, None]).astype(jnp.float32)
    listed = jnp.any(named, -1)
    logits = jnp.where(listed, table, -1e30)
    peak = jnp.max(logits, 0, keepdims=True)
    expo = jnp.exp(logits - peak)
    total = jnp.sum(expo, 0, keepdims=True)
    total_queries = candidates.shape[0]
    losses = peak[0] + jnp.log(total[0]) - jnp.sum(table * first, 0)
    loss = jnp.mean(losses)
    grad_table = (expo / total - first) / total_queries
    own = lax.dynamic_slice_in_dim(grad_table, me * NSEG, NSEG, 0)
    per_token = jnp.repeat(own, qlen, axis=1) / totals
    spots = jnp.sum(segmask[:, :, None] * per_token[:, None, :], 0)
    sim_low = (weight * spots).astype(jnp.bfloat16)
    query_grad = lax.dot_general(
        sim_low, doc_low, (((0,), (0,)), ((), ())), preferred_element_type=jnp.float32
    ).reshape(devices, qtok, pdim)
    query_local = lax.all_to_all(query_grad, AXES, 0, 0, tiled=True)
    doc_grad = jnp.dot(sim_low, rows_all, preferred_element_type=jnp.float32)

    *doc_out, doc_packed = backward_call(doc_grad, doc_seg, doc_kept, mats, vec_row)
    *query_out, query_packed = backward_call(query_local, query_seg, query_kept, mats, vec_row)
    inputs = ((doc_in, query_in),) + tuple((doc_kept[n], query_kept[n]) for n in (3, 5, 7, 9))
    acts = [
        v for (dx, qx), dy, qy in zip(inputs, doc_out, query_out) for v in (dx, qx, dy, qy)
    ]
    edges = [0]
    for m, _ in sizes:
        edges.append(edges[-1] + m)
    bounds = list(zip(edges[:-1], edges[1:]))
    side = doc_packed.shape[1] // 8
    span = edges[-1] + side
    span += -span % (128 * devices) if devices <= 32 else -span % (16 * devices)
    a_grads, b_grads, left = pl.pallas_call(
        grads_kernel,
        grid_spec=pltpu.PrefetchScalarGridSpec(
            num_scalar_prefetch=1,
            grid=(1,),
            in_specs=[whole(v) for v in acts + [fac_parts, early, doc_packed, query_packed]],
            out_specs=[
                pl.BlockSpec((4, 576, D), lambda i, me: (0, 0, 0)),
                pl.BlockSpec((4, 608, D), lambda i, me: (0, 0, 0)),
                pl.BlockSpec((8, span), lambda i, me: (0, 0)),
            ],
        ),
        out_shape=[
            jax.ShapeDtypeStruct((4, 576, D), jnp.bfloat16),
            jax.ShapeDtypeStruct((4, 608, D), jnp.bfloat16),
            jax.ShapeDtypeStruct((8, span), jnp.float32),
        ],
        name="grads",
    )(me_stream, *acts, fac_parts, early, doc_packed, query_packed)
    got = [exchange(a_grads[2:], 1), exchange(b_grads[2:], 2)]
    half = [add(a_grads[:2], got[0]), add(b_grads[:2], got[1])]

    summed = join_pieces(sum_piece(left))
    summed, half = lax.optimization_barrier((summed, half))
    got = [exchange(half[0][1], 2), exchange(half[1][1], 1)]
    full = [add(half[0][0], got[0]), add(half[1][0], got[1])]

    wide += -wide % (128 * devices) if devices <= 32 else -wide % (128 * devices // 8)
    basis, right = pl.pallas_call(
        lambda *refs: factors_kernel(bounds, *refs),
        grid_spec=pltpu.PrefetchScalarGridSpec(
            num_scalar_prefetch=1,
            grid=(1,),
            in_specs=[whole(summed)]
            + [whole(v) for v in acts]
            + [
                pl.BlockSpec((e.shape[0] // 4, e.shape[1]), lambda i, me: (me[0], 0))
                for e in errs[:4]
            ]
            + [whole(errs[4])],
            out_specs=[
                pl.BlockSpec((8, edges[-1]), lambda i, me: (0, 0)),
                pl.BlockSpec((8, wide), lambda i, me: (0, 0)),
            ],
        ),
        out_shape=[
            jax.ShapeDtypeStruct((8, edges[-1]), jnp.float32),
            jax.ShapeDtypeStruct((8, wide), jnp.float32),
        ],
        name="factors",
    )(me_stream, summed, *acts, *errs)
    right, full = lax.optimization_barrier((right, full))
    got = [exchange(full[0], 2), exchange(full[1], 1)]
    mine = sum_piece(right)
    pair = [jnp.stack([one, two], 0) for one, two in zip(full, got)]
    mine, pair = lax.optimization_barrier((mine, pair))
    last = [exchange(pair[0], 1), exchange(pair[1], 2)]
    joined = join_pieces(mine)
    sums = (pair[0], last[0], pair[1], last[1])
    rights, spans, at = [], [], 0
    for _, n in sizes:
        rights.append(joined[:, at : at + n])
        spans.append((at, n))
        at += n

    rate = RATE * qdev * math.sqrt(devices / (row + qtok))
    firsts, seconds = thirds(basis), thirds(joined)
    left_parts = jnp.concatenate([firsts[k] for k in (0, 0, 1, 0, 1, 2)], 0).T
    right_parts = jnp.concatenate([seconds[k] for k in (0, 1, 0, 2, 1, 0)], 0)
    left_parts = [left_parts[lo:hi] for lo, hi in bounds]
    steps = 6

    def part_spec(value, head):
        if head:
            return pl.BlockSpec(value.shape, lambda i: (0, 0))
        return pl.BlockSpec((value.shape[0] // steps, value.shape[1]), lambda i: (i, 0))

    trios = list(zip(left_parts, moms, weights))
    moved = pl.pallas_call(
        lambda *refs: weight_kernel(spans, rate, *refs),
        grid=(steps,),
        in_specs=[part_spec(v, True) for v in (right_parts, summed, vec_row, vec_row)]
        + [part_spec(v, n == 4) for n, trio in enumerate(trios) for v in trio],
        out_specs=[part_spec(w, n == 4) for n, w in enumerate(weights) for _ in range(2)]
        + [part_spec(vec_row, True)] * 2,
        out_shape=[jax.ShapeDtypeStruct(w.shape, jnp.float32) for w in weights for _ in range(2)]
        + [jax.ShapeDtypeStruct(vec_row.shape, jnp.float32)] * 2,
        name="weights",
    )(right_parts, summed, vec_row, mom_vectors[None, :], *[v for trio in trios for v in trio])
    new_w, new_m = list(moved[0:10:2]), list(moved[1:10:2])
    new_w[4], new_m[4] = new_w[4].T, new_m[4].T
    new_vec, vec_mom = moved[10][0], moved[11][0]

    def quartered(value):
        if value.shape[0] == 4 * D:
            return value.reshape(4, D, value.shape[1])
        return value

    def quarter_spec(value):
        if len(value.shape) == 3:
            return pl.BlockSpec((4, D // 4, value.shape[2]), lambda q, me: (0, q, 0))
        if value.shape[0] != D or value is left_parts[4]:
            return pl.BlockSpec(value.shape, lambda q, me: (0, 0))
        return pl.BlockSpec((D // 4, value.shape[1]), lambda q, me: (q, 0))

    rows = [quartered(v) for v in left_parts] + [quartered(v) for v in errs]
    out = [jax.ShapeDtypeStruct(quartered(e).shape, jnp.float32) for e in errs]
    new_e = pl.pallas_call(
        lambda *refs: error_kernel(spans, replicas, *refs),
        grid_spec=pltpu.PrefetchScalarGridSpec(
            num_scalar_prefetch=1,
            grid=(4,),
            in_specs=[
                pl.BlockSpec(right_parts.shape, lambda q, me: (0, 0)),
                pl.BlockSpec((1, 576, D), lambda q, me: ((q ^ me[0]) >> 1, 0, 0)),
                pl.BlockSpec((1, 576, D), lambda q, me: ((q ^ me[0]) >> 1, 0, 0)),
                pl.BlockSpec((1, 608, D), lambda q, me: ((q ^ me[0]) & 1, 0, 0)),
                pl.BlockSpec((1, 608, D), lambda q, me: ((q ^ me[0]) & 1, 0, 0)),
            ]
            + [quarter_spec(v) for v in rows],
            out_specs=[quarter_spec(v) for v in out],
        ),
        out_shape=out,
        name="errors",
    )(me_stream, right_parts, *sums, *rows)
    new_e = [v.reshape((1,) + e.shape) for v, e in zip(new_e, errs)]
    new_e[4] = jnp.swapaxes(new_e[4], 1, 2)
    return (
        loss,
        *new_w,
        new_vec,
        *new_m,
        vec_mom,
        *new_e,
        *[right.T for right in rights],
    )


def solution(mesh):
    return jax.shard_map(
        shards,
        mesh=mesh,
        in_specs=(
            P(("stream", "replica"), None, None),
            P(("stream", "replica"), None, None),
            P(("stream", "replica"), None),
            P(),
            P(),
            P(),
            P(),
            P(),
            P(),
            P(),
            P(),
            P(),
            P(),
            P(),
            P(),
            P(),
            P(),
            P("replica", None, None),
            P("replica", None, None),
            P("replica", None, None),
            P("replica", None, None),
            P("replica", None, None),
            P(),
            P(),
            P(),
            P(),
            P(),
        ),
        out_specs=(
            P(),
            P(),
            P(),
            P(),
            P(),
            P(),
            P(),
            P(),
            P(),
            P(),
            P(),
            P(),
            P(),
            P("replica", None, None),
            P("replica", None, None),
            P("replica", None, None),
            P("replica", None, None),
            P("replica", None, None),
            P(),
            P(),
            P(),
            P(),
            P(),
        ),
        check_vma=False,
    )
```
